32 devices in a mesh: parts: 2 (over x), seq: 16 (over z, y, core).
Axes of the slice: x: 2, y: 2, z: 4, core: 2. Of those that a mesh axis runs over, the one named last changes fastest.
Arguments:
- control: bfloat16 [256, 3072], P(('parts', 'seq')), parts along dimension 0, may hold values from -6 to 6
- mask_ids: int32 [256], P(('parts', 'seq')), parts along dimension 0, may hold values from 0 to 2
- owner: int32 [256], P('parts'), parts along dimension 0, may hold values from 0 to 127, each once
- mask_table: bfloat16 [3, 3072], replicated, may hold values from -6 to 6
- res_weight: bfloat16 [3072, 3072], P(None, 'seq'), may hold values from -0.109375 to 0.109375
- base: bfloat16 [256, 3072], P(('parts', 'seq')), parts along dimension 0, may hold values from -6 to 6
- modulation: float32 [2, 3072], replicated, may hold values from -0.5 to 0.5
- q_weight: bfloat16 [3072, 1536], P(None, 'seq'), may hold values from -1 to 1
- k_weight: bfloat16 [3072, 1536], P(None, 'seq'), may hold values from -4 to 4
- v_weight: bfloat16 [3072, 1536], P(None, 'seq'), may hold values from -0.109375 to 0.109375
Outputs:
- hidden_out: bfloat16 [256, 3072], P(('parts', 'seq')), parts along dimension 0
- attended: bfloat16 [256, 1536], P(('parts', 'seq')), parts along dimension 0
The draws below stay inside these ranges and needn't reach their ends.
There are 2 independent parts, one for each index of `parts`. The reference program is written for one: setup_inputs(seed, part) draws one part's arguments, and reference() takes and returns one part's arrays. A program takes and returns all parts, laid end to end along the dimension named above; an argument that names none is the same for every part. Nothing has to cross between parts.
Inputs may be any that keep to these rules, and one draw needn't show every extreme that they name: `owner`: each base row is named by exactly one control row.
All inputs are finite; a program needn't handle non-finite values.
Results may differ from the reference program's by a relative error of at most 0.006.
Values may be sent and summed in bfloat16 or wider, within the bound.
No kernel may reach another device: no remote copies, remote signals or barrier semaphores. Data moves between devices by JAX's collectives and lax.ppermute only.
A program may use at most 64 MiB of HBM per device.

```python
import math
import jax
import jax.numpy as jnp
from jax import lax

D = 3072
HEADS = 12
HEAD_DIM = 128
MASK_KINDS = 3
TOKENS = 128
HD = 1536


def shared_query(key):
    return jax.random.normal(jax.random.fold_in(key, 11), (D, HEADS * HEAD_DIM), jnp.float32) / math.sqrt(D)


def draw_q_weight(key, part):
    return jnp.clip(shared_query(key), -1.0, 1.0).astype(jnp.bfloat16)


def draw_k_weight(key, part):
    jitter = jax.random.normal(jax.random.fold_in(key, 12), (D, HEADS * HEAD_DIM), jnp.float32) / math.sqrt(D)
    mixed = jitter
    return jnp.clip(mixed, -4.0, 4.0).astype(jnp.bfloat16)


def place_ends(values, stream_key, low, top_value):
    spot = [jax.random.randint(jax.random.fold_in(stream_key, axis), (), 0, length) for axis, length in enumerate(values.shape)]
    widest = values.shape.index(max(values.shape))
    next_to = spot[:widest] + [(spot[widest] + 1) % values.shape[widest]] + spot[widest + 1:]
    return values.at[tuple(spot)].set(low).at[tuple(next_to)].set(top_value)


def block_scale(own_key, extent, shards, least, top_value):
    def one(axis_at, parts):
        heights = jax.random.uniform(jax.random.fold_in(jax.random.fold_in(own_key, 6), axis_at), (parts,), jnp.float32, least / len(shards), top_value / len(shards))
        return jnp.repeat(jnp.exp(heights), extent[axis_at] // parts).reshape((-1,) + (1,) * (len(extent) - axis_at - 1))

    level = one(*shards[0])
    for cut in shards[1:]:
        level = level * one(*cut)
    return level


def bell_draw(stream_key, shape, deviation, reach, pieces=(), held_as=jnp.bfloat16):
    drawn = deviation * jax.random.normal(stream_key, shape, jnp.float32)
    if pieces:
        drawn = drawn * block_scale(stream_key, shape, pieces, -0.22, 0.18)
    return jnp.clip(drawn, -reach, reach).astype(held_as)


def setup_inputs(seed: int = 0, part: int = 0) -> dict:
    streams_of = jax.random.split(jax.random.key(seed), 11)
    part_splits = jax.random.split(jax.random.fold_in(streams_of[10], part), 11)
    return {
        "control": bell_draw(part_splits[0], (TOKENS, D), 1.0, 6.0, ((0, 16),)),
        "mask_ids": place_ends(jax.random.randint(part_splits[1], (TOKENS,), 0, MASK_KINDS), jax.random.fold_in(part_splits[1], 1), 0, MASK_KINDS - 1).astype(jnp.int32),
        "owner": jax.random.permutation(part_splits[2], TOKENS).astype(jnp.int32),
        "mask_table": bell_draw(streams_of[3], (MASK_KINDS, D), 1.0, 6.0),
        "res_weight": bell_draw(streams_of[4], (D, D), D ** -0.5, 0.109375, ((1, 16),)),
        "base": bell_draw(part_splits[5], (TOKENS, D), 1.0, 6.0, ((0, 16),)),
        "modulation": jnp.clip(jax.random.uniform(streams_of[6], (2, D), jnp.float32, -0.5, 0.5), -0.5, 0.5),
        "q_weight": draw_q_weight(jax.random.fold_in(streams_of[10], 71), part),
        "k_weight": draw_k_weight(jax.random.fold_in(streams_of[10], 71), part),
        "v_weight": bell_draw(streams_of[9], (D, HD), D ** -0.5, 0.109375, ((1, 16),)),
    }


def layer_norm(hidden, modulation):
    row_mean = lax.optimization_barrier(jnp.mean(hidden, axis=1, keepdims=True))
    centred = hidden - row_mean
    row_var = lax.optimization_barrier(jnp.mean(centred * centred, axis=1, keepdims=True))
    scaled = centred * lax.rsqrt(row_var + 1e-06)
    return (scaled * (1.0 + modulation[1]) + modulation[0]).astype(jnp.bfloat16)

def one_head(head_args):
    query_head, key_head, value_head = head_args
    scores = jnp.dot(query_head, key_head.T, precision=lax.Precision.HIGHEST, preferred_element_type=jnp.float32) / math.sqrt(HEAD_DIM)
    expo = jnp.exp(scores - lax.optimization_barrier(jnp.max(scores, axis=1, keepdims=True)))
    denom = lax.optimization_barrier(jnp.sum(expo, axis=1, keepdims=True))
    probs = expo.astype(jnp.bfloat16).astype(jnp.float32)
    return jnp.dot(probs, value_head, precision=lax.Precision.HIGHEST, preferred_element_type=jnp.float32) / denom

def split_heads(matrix):
    return matrix.astype(jnp.float32).reshape(TOKENS, HEADS, HEAD_DIM).transpose(1, 0, 2)

def reference(control, mask_ids, owner, mask_table, res_weight, base, modulation, q_weight, k_weight, v_weight):
    selector = (mask_ids[:, None] == jnp.arange(MASK_KINDS, dtype=jnp.int32)[None, :]).astype(jnp.bfloat16)
    condition = (control.astype(jnp.float32) + jnp.dot(selector, mask_table, preferred_element_type=jnp.float32)).astype(jnp.bfloat16)
    residual = jnp.dot(condition, res_weight, preferred_element_type=jnp.float32).astype(jnp.bfloat16)
    inverse = jnp.zeros((TOKENS,), jnp.int32).at[owner].set(jnp.arange(TOKENS, dtype=jnp.int32))
    relayed = jnp.take(residual, inverse, axis=0)
    hidden = base.astype(jnp.float32) + relayed.astype(jnp.float32)
    normed = layer_norm(hidden, modulation)
    queries = jnp.dot(normed, q_weight, preferred_element_type=jnp.float32).astype(jnp.bfloat16)
    key_rows = jnp.dot(normed, k_weight, preferred_element_type=jnp.float32).astype(jnp.bfloat16)
    values = jnp.dot(normed, v_weight, preferred_element_type=jnp.float32).astype(jnp.bfloat16)
    outputs = lax.map(one_head, (split_heads(queries), split_heads(key_rows), split_heads(values)))
    attended = outputs.transpose(1, 0, 2).reshape(TOKENS, HEADS * HEAD_DIM).astype(jnp.bfloat16)
    return (hidden.astype(jnp.bfloat16), attended)
```

```python
import functools
import math

import jax
import jax.numpy as jnp
from jax import lax
from jax.sharding import PartitionSpec as P

HEAD_DIM = 128


def ring_order(devices):
    chips = devices // 2
    narrow = 1
    while (2 * narrow) ** 2 <= chips and chips % (2 * narrow) == 0:
        narrow *= 2
    long = chips // narrow
    if narrow == 1:
        walk = [(row, 0) for row in range(long)]
    else:
        walk = [(row, 0) for row in range(long)]
        for back, row in enumerate(reversed(range(long))):
            columns = range(1, narrow) if back % 2 == 0 else range(narrow - 1, 0, -1)
            walk += [(row, column) for column in columns]
    return [(row * narrow + column) * 2 + core for row, column in walk for core in range(2)]


def layer_norm(hidden, modulation):
    row_mean = jnp.mean(hidden, axis=1, keepdims=True)
    centred = hidden - row_mean
    row_var = jnp.mean(centred * centred, axis=1, keepdims=True)
    scaled = centred * lax.rsqrt(row_var + 1e-06)
    return (scaled * (1.0 + modulation[1]) + modulation[0]).astype(jnp.bfloat16)


def on_device(
    devices,
    control,
    mask_ids,
    owner,
    mask_table,
    res_weight,
    base,
    modulation,
    q_weight,
    k_weight,
    v_weight,
):
    row_count = base.shape[0]
    total_rows = owner.shape[0]
    width = q_weight.shape[1]
    ring = ring_order(devices)
    team = math.lcm(width, HEAD_DIM) // width
    teams = devices // team
    team_heads = team * width // HEAD_DIM
    me = lax.axis_index("seq")
    place = me % team

    selector = (
        mask_ids[:, None] == jnp.arange(mask_table.shape[0], dtype=jnp.int32)[None, :]
    ).astype(jnp.bfloat16)
    condition = (
        control.astype(jnp.float32)
        + jnp.dot(selector, mask_table, preferred_element_type=jnp.float32)
    ).astype(jnp.bfloat16)
    conditions = lax.all_gather(condition, "seq", axis=0, tiled=True, axis_index_groups=[ring])
    residual = jnp.dot(conditions, res_weight, preferred_element_type=jnp.float32).astype(
        jnp.bfloat16
    )
    owner_ring = jnp.concatenate(
        [owner[place_ * row_count : (place_ + 1) * row_count] for place_ in ring]
    )
    relay = (jnp.arange(total_rows, dtype=jnp.int32)[:, None] == owner_ring[None, :]).astype(
        jnp.bfloat16
    )
    by_owner = jnp.dot(relay, residual, preferred_element_type=jnp.float32).astype(jnp.bfloat16)
    relayed = lax.all_to_all(by_owner, "seq", split_axis=0, concat_axis=1, tiled=True)
    hidden = base.astype(jnp.float32) + relayed.astype(jnp.float32)
    normed = layer_norm(hidden, modulation)
    joined = jnp.concatenate([q_weight, k_weight, v_weight], axis=1)
    normed_all = lax.all_gather(normed, "seq", axis=0, tiled=True, axis_index_groups=[ring])
    columns = lax.dot_general(
        joined, normed_all, (((0,), (1,)), ((), ())), preferred_element_type=jnp.float32
    ).astype(jnp.bfloat16)
    team_groups = [[t * team + r for r in range(team)] for t in range(teams)]
    columns = lax.all_gather(columns, "seq", axis=0, axis_index_groups=team_groups)
    columns = columns.reshape(team, 3, width, total_rows).transpose(1, 0, 2, 3)
    columns = columns.reshape(3, team_heads, HEAD_DIM, total_rows)
    spots = jnp.array([ring.index(d) for d in range(devices)], jnp.int32).reshape(teams, team)
    blocks = columns[0].reshape(team_heads, HEAD_DIM, devices, row_count)
    queries = jnp.take(blocks, jnp.take(spots, place, axis=1), axis=2)
    queries = queries.reshape(team_heads, HEAD_DIM, teams * row_count)
    scores = jnp.einsum(
        "hdt,hdk->htk", queries, columns[1], preferred_element_type=jnp.float32
    ) / math.sqrt(HEAD_DIM)
    expo = jnp.exp(scores - jnp.max(scores, axis=2, keepdims=True))
    denom = jnp.sum(expo, axis=2)
    summed = jnp.einsum(
        "htk,hdk->thd",
        expo.astype(jnp.bfloat16),
        columns[2],
        preferred_element_type=jnp.float32,
    )
    mine = (summed / denom.T[:, :, None]).astype(jnp.bfloat16)
    mine = mine.reshape(teams, row_count, team_heads * HEAD_DIM)
    place_groups = [[t * team + r for t in range(teams)] for r in range(team)]
    parts = lax.all_to_all(
        mine, "seq", split_axis=0, concat_axis=0, tiled=True, axis_index_groups=place_groups
    )
    attended = parts.transpose(1, 0, 2).reshape(row_count, teams * team_heads * HEAD_DIM)
    return (hidden.astype(jnp.bfloat16), attended)


def solution(mesh):
    in_specs = (
        P(("parts", "seq"), None),
        P(("parts", "seq")),
        P("parts"),
        P(),
        P(None, "seq"),
        P(("parts", "seq"), None),
        P(),
        P(None, "seq"),
        P(None, "seq"),
        P(None, "seq"),
    )
    out_specs = (P(("parts", "seq"), None), P(("parts", "seq"), None))
    return jax.shard_map(
        functools.partial(on_device, mesh.shape["seq"]),
        mesh=mesh,
        in_specs=in_specs,
        out_specs=out_specs,
        check_vma=False,
    )
```

```python
import functools
import math

import jax
import jax.numpy as jnp
from jax import lax
from jax.experimental import pallas as pl
from jax.experimental.pallas import tpu as pltpu
from jax.sharding import PartitionSpec as P

HEAD_DIM = 128


def ring_order(devices):
    chips = devices // 2
    narrow = 1
    while (2 * narrow) ** 2 <= chips and chips % (2 * narrow) == 0:
        narrow *= 2
    long = chips // narrow
    if narrow == 1:
        walk = [(row, 0) for row in range(long)]
    else:
        walk = [(row, 0) for row in range(long)]
        for back, row in enumerate(reversed(range(long))):
            columns = range(1, narrow) if back % 2 == 0 else range(narrow - 1, 0, -1)
            walk += [(row, column) for column in columns]
    return [(row * narrow + column) * 2 + core for row, column in walk for core in range(2)]


def layer_norm(hidden, modulation):
    row_mean = jnp.mean(hidden, axis=1, keepdims=True)
    centred = hidden - row_mean
    row_var = jnp.mean(centred * centred, axis=1, keepdims=True)
    scaled = centred * lax.rsqrt(row_var + 1e-06)
    return (scaled * (1.0 + modulation[1]) + modulation[0]).astype(jnp.bfloat16)


def on_device_plain(
    devices,
    control,
    mask_ids,
    owner,
    mask_table,
    res_weight,
    base,
    modulation,
    q_weight,
    k_weight,
    v_weight,
):
    row_count = base.shape[0]
    total_rows = owner.shape[0]
    width = q_weight.shape[1]
    ring = ring_order(devices)
    team = math.lcm(width, HEAD_DIM) // width
    teams = devices // team
    team_heads = team * width // HEAD_DIM
    me = lax.axis_index("seq")
    place = me % team

    selector = (
        mask_ids[:, None] == jnp.arange(mask_table.shape[0], dtype=jnp.int32)[None, :]
    ).astype(jnp.bfloat16)
    condition = (
        control.astype(jnp.float32)
        + jnp.dot(selector, mask_table, preferred_element_type=jnp.float32)
    ).astype(jnp.bfloat16)
    conditions = lax.all_gather(condition, "seq", axis=0, tiled=True, axis_index_groups=[ring])
    residual = jnp.dot(conditions, res_weight, preferred_element_type=jnp.float32).astype(
        jnp.bfloat16
    )
    owner_ring = jnp.concatenate(
        [owner[place_ * row_count : (place_ + 1) * row_count] for place_ in ring]
    )
    relay = (jnp.arange(total_rows, dtype=jnp.int32)[:, None] == owner_ring[None, :]).astype(
        jnp.bfloat16
    )
    by_owner = jnp.dot(relay, residual, preferred_element_type=jnp.float32).astype(jnp.bfloat16)
    relayed = lax.all_to_all(by_owner, "seq", split_axis=0, concat_axis=1, tiled=True)
    hidden = base.astype(jnp.float32) + relayed.astype(jnp.float32)
    normed = layer_norm(hidden, modulation)
    joined = jnp.concatenate([q_weight, k_weight, v_weight], axis=1)
    normed_all = lax.all_gather(normed, "seq", axis=0, tiled=True, axis_index_groups=[ring])
    columns = lax.dot_general(
        joined, normed_all, (((0,), (1,)), ((), ())), preferred_element_type=jnp.float32
    ).astype(jnp.bfloat16)
    team_groups = [[t * team + r for r in range(team)] for t in range(teams)]
    columns = lax.all_gather(columns, "seq", axis=0, axis_index_groups=team_groups)
    columns = columns.reshape(team, 3, width, total_rows).transpose(1, 0, 2, 3)
    columns = columns.reshape(3, team_heads, HEAD_DIM, total_rows)
    spots = jnp.array([ring.index(d) for d in range(devices)], jnp.int32).reshape(teams, team)
    blocks = columns[0].reshape(team_heads, HEAD_DIM, devices, row_count)
    queries = jnp.take(blocks, jnp.take(spots, place, axis=1), axis=2)
    queries = queries.reshape(team_heads, HEAD_DIM, teams * row_count)
    scores = jnp.einsum(
        "hdt,hdk->htk", queries, columns[1], preferred_element_type=jnp.float32
    ) / math.sqrt(HEAD_DIM)
    expo = jnp.exp(scores - jnp.max(scores, axis=2, keepdims=True))
    denom = jnp.sum(expo, axis=2)
    summed = jnp.einsum(
        "htk,hdk->thd",
        expo.astype(jnp.bfloat16),
        columns[2],
        preferred_element_type=jnp.float32,
    )
    mine = (summed / denom.T[:, :, None]).astype(jnp.bfloat16)
    mine = mine.reshape(teams, row_count, team_heads * HEAD_DIM)
    place_groups = [[t * team + r for t in range(teams)] for r in range(team)]
    parts = lax.all_to_all(
        mine, "seq", split_axis=0, concat_axis=0, tiled=True, axis_index_groups=place_groups
    )
    attended = parts.transpose(1, 0, 2).reshape(row_count, teams * team_heads * HEAD_DIM)
    return (hidden.astype(jnp.bfloat16), attended)


VMEM = pl.BlockSpec(memory_space=pltpu.VMEM)
SMEM = pl.BlockSpec(memory_space=pltpu.SMEM)
HBM = pl.BlockSpec(memory_space=pltpu.HBM)
NT = (((1,), (1,)), ((), ()))
STAT_ROWS = 16


def call(kernel, out_shape, in_specs, scratch=(), limit=8 << 20):
    multiple = isinstance(out_shape, (tuple, list))
    return pl.pallas_call(
        kernel,
        out_shape=out_shape,
        in_specs=in_specs,
        out_specs=[VMEM] * len(out_shape) if multiple else VMEM,
        scratch_shapes=list(scratch),
        compiler_params=pltpu.CompilerParams(vmem_limit_bytes=limit),
    )


def matmul_nt(left, right):
    return lax.dot_general(left, right, NT, preferred_element_type=jnp.float32)


def identity(size):
    rows = lax.broadcasted_iota(jnp.int32, (size, size), 0)
    return (rows == lax.broadcasted_iota(jnp.int32, (size, size), 1)).astype(jnp.bfloat16)


def condition_kernel(
    far_ids,
    far_control,
    far_table,
    far_base,
    far_weight,
    far_owner,
    condition,
    pieces,
    weight,
    owner,
    ids,
    control,
    table,
    base,
    arrived,
):
    copies = [
        pltpu.make_async_copy(source, target, arrived.at[i])
        for i, (source, target) in enumerate(
            (
                (far_base, base),
                (far_ids, ids),
                (far_table, table),
                (far_control, control),
                (far_owner, owner),
                (far_weight, weight),
            )
        )
    ]
    for copy in copies:
        copy.start()
    rows, model = control.shape
    kinds = table.shape[0]
    devices, _, block = pieces.shape
    copies[0].wait()
    for d in range(devices):
        pieces[d] = base[:, d * block : (d + 1) * block]
    copies[1].wait()
    kind = jnp.zeros((rows, 1), jnp.int32)
    row = lax.broadcasted_iota(jnp.int32, (rows, 1), 0)
    for i in range(rows):
        kind = jnp.where(row == i, ids[i], kind)
    copies[2].wait()
    copies[3].wait()
    entries = table[...].astype(jnp.float32)
    chosen = jnp.broadcast_to(entries[:1], (rows, model))
    for j in range(1, kinds):
        chosen = jnp.where(kind == j, entries[j : j + 1], chosen)
    condition[...] = (control[...].astype(jnp.float32) + chosen).astype(jnp.bfloat16)
    copies[4].wait()
    copies[5].wait()


def residual_kernel(ring, conditions, weight, owner, base, out):
    rows = conditions.shape[0]
    block = weight.shape[0]
    count = rows // len(ring)
    residual = matmul_nt(weight[...], conditions[...]).astype(jnp.bfloat16)
    row = lax.broadcasted_iota(jnp.int32, (rows, rows), 0)
    names = (row == owner[...]).astype(jnp.bfloat16)
    lane = lax.broadcasted_iota(jnp.int32, (1, rows), 1)
    holder = jnp.zeros((1, rows), jnp.int32)
    for s, device in enumerate(ring):
        holder = jnp.where(lane // count == s, device, holder)
    turned = (row == holder * count + lane % count).astype(jnp.bfloat16)
    relay = jnp.dot(names, turned, preferred_element_type=jnp.float32).astype(jnp.bfloat16)
    own = base[...].astype(jnp.float32).reshape(rows, block).astype(jnp.bfloat16)
    hidden = matmul_nt(residual, relay) + matmul_nt(identity(block), own)
    middle = jnp.mean(hidden, axis=0, keepdims=True)
    apart = hidden - middle
    squares = jnp.sum(apart * apart, axis=0, keepdims=True)
    out[:block] = apart.astype(jnp.bfloat16)
    line = lax.broadcasted_iota(jnp.int32, (STAT_ROWS, rows), 0)
    stats = jnp.zeros((STAT_ROWS, rows), jnp.float32)
    for first, value in ((0, middle), (3, squares)):
        for term in range(3):
            head = value.astype(jnp.bfloat16).astype(jnp.float32)
            stats = jnp.where(line == first + term, head, stats)
            value = value - head
    out[block:] = stats.astype(jnp.bfloat16)


def project_kernel(
    ring, me, gathered, modulation, q_weight, k_weight, v_weight, columns, hidden_out, normed, turned
):
    devices = len(ring)
    rows = gathered.shape[1]
    stride = gathered.shape[0] // devices
    block = stride - STAT_ROWS
    model = block * devices
    count = hidden_out.shape[0]
    width = q_weight.shape[0]
    middles, squares = [], jnp.zeros((1, rows), jnp.float32)
    for s in range(devices):
        stats = gathered[s * stride + block : (s + 1) * stride].astype(jnp.float32)
        middles.append(stats[0:1] + stats[1:2] + stats[2:3])
        squares = squares + (stats[3:4] + stats[4:5] + stats[5:6])
    mean = sum(middles) * (1.0 / devices)
    offsets = [middle - mean for middle in middles]
    for offset in offsets:
        squares = squares + block * (offset * offset)
    inverse = lax.rsqrt(squares * (1.0 / model) + 1e-06)
    table = jnp.concatenate(
        offsets + [inverse, mean, jnp.zeros((rows - devices - 2, rows), jnp.float32)], axis=0
    )
    turned[...] = table.T
    inverse_column = turned[:, devices : devices + 1]
    first = pl.multiple_of(me[0] * count, count)
    mine = turned[pl.ds(first, count), :]
    eye = identity(rows)
    own_row = lax.broadcasted_iota(jnp.int32, (count, rows), 0) + first
    pick = (own_row == lax.broadcasted_iota(jnp.int32, (count, rows), 1)).astype(jnp.bfloat16)
    pair = 2 * block
    side = lax.broadcasted_iota(jnp.int32, (1, pair), 1) < block
    for p in range(devices // 2):
        lanes = slice(ring[2 * p] * block, ring[2 * p] * block + pair)
        start = 2 * p * stride
        apart = jnp.concatenate(
            [gathered[start : start + block], gathered[start + stride : start + stride + block]],
            axis=0,
        )
        centred = matmul_nt(eye, apart) + jnp.where(
            side, turned[:, 2 * p : 2 * p + 1], turned[:, 2 * p + 1 : 2 * p + 2]
        )
        scaled = (centred * inverse_column) * (1.0 + modulation[1:2, lanes])
        normed[:, lanes] = (scaled + modulation[0:1, lanes]).astype(jnp.bfloat16)
        own = matmul_nt(pick, apart) + jnp.where(
            side, mine[:, 2 * p : 2 * p + 1], mine[:, 2 * p + 1 : 2 * p + 2]
        )
        hidden_out[:, lanes] = (own + mine[:, devices + 1 : devices + 2]).astype(jnp.bfloat16)
    for j, weight in enumerate((q_weight, k_weight, v_weight)):
        columns[j * width : (j + 1) * width] = matmul_nt(weight[...], normed[...]).astype(
            jnp.bfloat16
        )


def attend_kernel(place, gathered, out, queries, keys, values):
    team, tall, rows = gathered.shape
    width = tall // 3
    teams, count, _ = out.shape
    for r in range(team):
        span = slice(r * width, (r + 1) * width)
        queries[span] = gathered[r, :width]
        keys[span] = gathered[r, width : 2 * width]
        values[span] = gathered[r, 2 * width :]
    line = lax.broadcasted_iota(jnp.int32, (teams * count, rows), 0)
    wanted = ((line // count) * team + place[0]) * count + line % count
    pick = (wanted == lax.broadcasted_iota(jnp.int32, (teams * count, rows), 1)).astype(
        jnp.bfloat16
    )
    chosen = matmul_nt(pick, queries[...]).astype(jnp.bfloat16)
    for h in range(team * width // HEAD_DIM):
        span = slice(h * HEAD_DIM, (h + 1) * HEAD_DIM)
        scores = jnp.dot(
            chosen[:, span], keys[span], preferred_element_type=jnp.float32
        ) / math.sqrt(HEAD_DIM)
        expo = jnp.exp(scores - jnp.max(scores, axis=1, keepdims=True))
        denom = jnp.sum(expo, axis=1, keepdims=True)
        mixed = matmul_nt(expo.astype(jnp.bfloat16), values[span]) / denom
        out[:, :, span] = mixed.reshape(teams, count, HEAD_DIM).astype(jnp.bfloat16)


def on_device(
    devices,
    control,
    mask_ids,
    owner,
    mask_table,
    res_weight,
    base,
    modulation,
    q_weight,
    k_weight,
    v_weight,
):
    count, model = base.shape
    rows = owner.shape[0]
    block = res_weight.shape[1]
    width = q_weight.shape[1]
    ring = ring_order(devices)
    team = math.lcm(width, HEAD_DIM) // width
    teams = devices // team
    me = lax.axis_index("seq")
    bf16 = jnp.bfloat16
    shape = jax.ShapeDtypeStruct

    inputs = (mask_ids, control, mask_table, base, res_weight.T, owner.reshape(1, rows))
    condition, pieces, near_weight, near_owner = call(
        condition_kernel,
        (
            pltpu.VMEM((count, model), bf16),
            pltpu.HBM((devices, count, block), bf16),
            pltpu.VMEM((block, model), bf16),
            pltpu.VMEM((1, rows), jnp.int32),
        ),
        [HBM] * len(inputs),
        [
            pltpu.SMEM((count,), jnp.int32),
            pltpu.VMEM((count, model), bf16),
            pltpu.VMEM(mask_table.shape, bf16),
            pltpu.VMEM((count, model), bf16),
            pltpu.SemaphoreType.DMA((len(inputs),)),
        ],
    )(*[pltpu.with_memory_space_constraint(x, pltpu.HBM) for x in inputs])
    base_columns = lax.all_to_all(pieces, "seq", split_axis=0, concat_axis=0, tiled=True)
    conditions = lax.all_gather(condition, "seq", axis=0, tiled=True, axis_index_groups=[ring])
    payload = call(
        functools.partial(residual_kernel, ring),
        shape((block + STAT_ROWS, rows), bf16),
        [VMEM] * 4,
    )(conditions, near_weight, near_owner, base_columns)
    gathered = lax.all_gather(payload, "seq", axis=0, tiled=True, axis_index_groups=[ring])
    columns, hidden_out = call(
        functools.partial(project_kernel, ring),
        (shape((3 * width, rows), bf16), shape((count, model), bf16)),
        [SMEM] + [VMEM] * 5,
        [pltpu.VMEM((rows, model), bf16), pltpu.VMEM((rows, rows), jnp.float32)],
    )(me.reshape(1), gathered, modulation, q_weight.T, k_weight.T, v_weight.T)
    team_groups = [[t * team + r for r in range(team)] for t in range(teams)]
    columns = lax.all_gather(columns, "seq", axis=0, axis_index_groups=team_groups)
    head_columns = team * width
    mine = call(
        attend_kernel,
        shape((teams, count, head_columns), bf16),
        [SMEM, VMEM],
        [pltpu.VMEM((head_columns, rows), bf16)] * 3,
    )((me % team).reshape(1), columns)
    place_groups = [[t * team + r for t in range(teams)] for r in range(team)]
    parts = lax.all_to_all(
        mine, "seq", split_axis=0, concat_axis=0, tiled=True, axis_index_groups=place_groups
    )
    attended = parts.transpose(1, 0, 2).reshape(count, teams * head_columns)
    return (hidden_out, attended)


def fits(devices, rows, block, width):
    return rows == HEAD_DIM and devices % 2 == 0 and block % 64 == 0 and width % 16 == 0


def on_any_device(devices, *arguments):
    owner, res_weight, q_weight = arguments[2], arguments[4], arguments[7]
    tidy = fits(devices, owner.shape[0], res_weight.shape[1], q_weight.shape[1])
    return (on_device if tidy else on_device_plain)(devices, *arguments)


def solution(mesh):
    in_specs = (
        P(("parts", "seq"), None),
        P(("parts", "seq")),
        P("parts"),
        P(),
        P(None, "seq"),
        P(("parts", "seq"), None),
        P(),
        P(None, "seq"),
        P(None, "seq"),
        P(None, "seq"),
    )
    out_specs = (P(("parts", "seq"), None), P(("parts", "seq"), None))
    return jax.shard_map(
        functools.partial(on_any_device, mesh.shape["seq"]),
        mesh=mesh,
        in_specs=in_specs,
        out_specs=out_specs,
        check_vma=False,
    )
```

```python
import functools
import math

import jax
import jax.numpy as jnp
from jax import lax
from jax.experimental import pallas as pl
from jax.experimental.pallas import tpu as pltpu
from jax.sharding import PartitionSpec as P

HEAD_DIM = 128


def ring_order(devices):
    chips = devices // 2
    narrow = 1
    while (2 * narrow) ** 2 <= chips and chips % (2 * narrow) == 0:
        narrow *= 2
    long = chips // narrow
    if narrow == 1:
        walk = [(row, 0) for row in range(long)]
    else:
        walk = [(row, 0) for row in range(long)]
        for back, row in enumerate(reversed(range(long))):
            columns = range(1, narrow) if back % 2 == 0 else range(narrow - 1, 0, -1)
            walk += [(row, column) for column in columns]
    return [(row * narrow + column) * 2 + core for row, column in walk for core in range(2)]


def layer_norm(hidden, modulation):
    row_mean = jnp.mean(hidden, axis=1, keepdims=True)
    centred = hidden - row_mean
    row_var = jnp.mean(centred * centred, axis=1, keepdims=True)
    scaled = centred * lax.rsqrt(row_var + 1e-06)
    return (scaled * (1.0 + modulation[1]) + modulation[0]).astype(jnp.bfloat16)


def on_device_plain(
    devices,
    control,
    mask_ids,
    owner,
    mask_table,
    res_weight,
    base,
    modulation,
    q_weight,
    k_weight,
    v_weight,
):
    row_count = base.shape[0]
    total_rows = owner.shape[0]
    width = q_weight.shape[1]
    ring = ring_order(devices)
    team = math.lcm(width, HEAD_DIM) // width
    teams = devices // team
    team_heads = team * width // HEAD_DIM
    me = lax.axis_index("seq")
    place = me % team

    selector = (
        mask_ids[:, None] == jnp.arange(mask_table.shape[0], dtype=jnp.int32)[None, :]
    ).astype(jnp.bfloat16)
    condition = (
        control.astype(jnp.float32)
        + jnp.dot(selector, mask_table, preferred_element_type=jnp.float32)
    ).astype(jnp.bfloat16)
    conditions = lax.all_gather(condition, "seq", axis=0, tiled=True, axis_index_groups=[ring])
    residual = jnp.dot(conditions, res_weight, preferred_element_type=jnp.float32).astype(
        jnp.bfloat16
    )
    owner_ring = jnp.concatenate(
        [owner[place_ * row_count : (place_ + 1) * row_count] for place_ in ring]
    )
    relay = (jnp.arange(total_rows, dtype=jnp.int32)[:, None] == owner_ring[None, :]).astype(
        jnp.bfloat16
    )
    by_owner = jnp.dot(relay, residual, preferred_element_type=jnp.float32).astype(jnp.bfloat16)
    relayed = lax.all_to_all(by_owner, "seq", split_axis=0, concat_axis=1, tiled=True)
    hidden = base.astype(jnp.float32) + relayed.astype(jnp.float32)
    normed = layer_norm(hidden, modulation)
    joined = jnp.concatenate([q_weight, k_weight, v_weight], axis=1)
    normed_all = lax.all_gather(normed, "seq", axis=0, tiled=True, axis_index_groups=[ring])
    columns = lax.dot_general(
        joined, normed_all, (((0,), (1,)), ((), ())), preferred_element_type=jnp.float32
    ).astype(jnp.bfloat16)
    team_groups = [[t * team + r for r in range(team)] for t in range(teams)]
    columns = lax.all_gather(columns, "seq", axis=0, axis_index_groups=team_groups)
    columns = columns.reshape(team, 3, width, total_rows).transpose(1, 0, 2, 3)
    columns = columns.reshape(3, team_heads, HEAD_DIM, total_rows)
    spots = jnp.array([ring.index(d) for d in range(devices)], jnp.int32).reshape(teams, team)
    blocks = columns[0].reshape(team_heads, HEAD_DIM, devices, row_count)
    queries = jnp.take(blocks, jnp.take(spots, place, axis=1), axis=2)
    queries = queries.reshape(team_heads, HEAD_DIM, teams * row_count)
    scores = jnp.einsum(
        "hdt,hdk->htk", queries, columns[1], preferred_element_type=jnp.float32
    ) / math.sqrt(HEAD_DIM)
    expo = jnp.exp(scores - jnp.max(scores, axis=2, keepdims=True))
    denom = jnp.sum(expo, axis=2)
    summed = jnp.einsum(
        "htk,hdk->thd",
        expo.astype(jnp.bfloat16),
        columns[2],
        preferred_element_type=jnp.float32,
    )
    mine = (summed / denom.T[:, :, None]).astype(jnp.bfloat16)
    mine = mine.reshape(teams, row_count, team_heads * HEAD_DIM)
    place_groups = [[t * team + r for t in range(teams)] for r in range(team)]
    parts = lax.all_to_all(
        mine, "seq", split_axis=0, concat_axis=0, tiled=True, axis_index_groups=place_groups
    )
    attended = parts.transpose(1, 0, 2).reshape(row_count, teams * team_heads * HEAD_DIM)
    return (hidden.astype(jnp.bfloat16), attended)


VMEM = pl.BlockSpec(memory_space=pltpu.VMEM)
SMEM = pl.BlockSpec(memory_space=pltpu.SMEM)
HBM = pl.BlockSpec(memory_space=pltpu.HBM)
NT = (((1,), (1,)), ((), ()))
LANES = 128
GATHER_BYTES = 1 << 20


def call(kernel, out_shape, in_specs, scratch=(), limit=8 << 20):
    multiple = isinstance(out_shape, (tuple, list))
    return pl.pallas_call(
        kernel,
        out_shape=out_shape,
        in_specs=in_specs,
        out_specs=[VMEM] * len(out_shape) if multiple else VMEM,
        scratch_shapes=list(scratch),
        compiler_params=pltpu.CompilerParams(vmem_limit_bytes=limit),
    )


def matmul_nt(left, right):
    return lax.dot_general(left, right, NT, preferred_element_type=jnp.float32)


def identity(size):
    rows = lax.broadcasted_iota(jnp.int32, (size, size), 0)
    return (rows == lax.broadcasted_iota(jnp.int32, (size, size), 1)).astype(jnp.bfloat16)


def condition_kernel(
    far_ids,
    far_control,
    far_table,
    far_base,
    far_owner,
    block,
    tail,
    owner,
    ids,
    table,
    control,
    base,
    arrived,
):
    copies = [
        pltpu.make_async_copy(source, target, arrived.at[i])
        for i, (source, target) in enumerate(
            (
                (far_ids, ids),
                (far_table, table),
                (far_control, control),
                (far_base, base),
                (far_owner, owner),
            )
        )
    ]
    for copy in copies:
        copy.start()
    rows, model = control.shape
    kinds = table.shape[0]
    head = block.shape[1] - model
    copies[0].wait()
    kind = jnp.zeros((rows, 1), jnp.int32)
    row = lax.broadcasted_iota(jnp.int32, (rows, 1), 0)
    for i in range(rows):
        kind = jnp.where(row == i, ids[i], kind)
    copies[1].wait()
    copies[2].wait()
    entries = table[...].astype(jnp.float32)
    chosen = jnp.broadcast_to(entries[:1], (rows, model))
    for j in range(1, kinds):
        chosen = jnp.where(kind == j, entries[j : j + 1], chosen)
    block[:, :model] = (control[...].astype(jnp.float32) + chosen).astype(jnp.bfloat16)
    copies[3].wait()
    block[:, model:] = base[:, :head]
    for tile in range(tail.shape[0] // rows):
        lanes = slice(head + tile * LANES, head + (tile + 1) * LANES)
        tail[tile * rows : (tile + 1) * rows] = base[:, lanes]
    copies[4].wait()


def residual_kernel(team, me, own, others, weight, owner, tail, out, conditions):
    rows, model = conditions.shape
    block = weight.shape[0]
    near = own.shape[0]
    count = near // team
    far = (rows - near) // near
    conditions[:near] = own[:, :model]
    conditions[near:] = others[:, :model]
    residual = matmul_nt(weight[...], conditions[...]).astype(jnp.bfloat16)
    lane = lax.broadcasted_iota(jnp.int32, (1, rows), 1)
    block_at = lane // count
    beyond = block_at - team
    step = jnp.where(beyond < 0, 0, beyond % far + 1)
    member = jnp.where(beyond < 0, block_at, beyond // far)
    holder = ((me[0] // team) ^ step) * team + member
    row = lax.broadcasted_iota(jnp.int32, (rows, rows), 0)
    names = (row == owner[...]).astype(jnp.bfloat16)
    turned = (row == holder * count + lane % count).astype(jnp.bfloat16)
    relay = jnp.dot(names, turned, preferred_element_type=jnp.float32).astype(jnp.bfloat16)
    out[:block] = matmul_nt(residual, relay).astype(jnp.bfloat16)
    out[block:] = tail[...]


def project_kernel(
    ring,
    team,
    me,
    gathered,
    own,
    others,
    modulation,
    q_weight,
    k_weight,
    v_weight,
    columns,
    hidden_out,
    hidden,
    normed,
):
    devices = len(ring)
    rows, model = hidden.shape
    stride = gathered.shape[0] // devices
    block = model // devices
    count = hidden_out.shape[0]
    width = q_weight.shape[0]
    head = own.shape[1] - model
    far = others.shape[0] // own.shape[0]
    my_team = me[0] // team
    for r in range(team):
        for k in range(far + 1):
            first = pl.multiple_of(((my_team ^ k) * team + r) * count, count)
            source, at = (own, r) if k == 0 else (others, r * far + k - 1)
            hidden[pl.ds(first, count), :head] = source[
                at * count : (at + 1) * count, model:
            ].astype(jnp.float32)
    for tile in range((stride - block) // count):
        lanes = slice(head + tile * LANES, head + (tile + 1) * LANES)
        for s, device in enumerate(ring):
            start = s * stride + block + tile * count
            hidden[device * count : (device + 1) * count, lanes] = gathered[
                start : start + count
            ].astype(jnp.float32)
    eye = identity(rows)
    pair = 2 * block
    spans = []
    total = jnp.zeros((rows, 1), jnp.float32)
    squares = jnp.zeros((rows, 1), jnp.float32)
    for p in range(devices // 2):
        lanes = slice(ring[2 * p] * block, ring[2 * p] * block + pair)
        spans.append(lanes)
        start = 2 * p * stride
        relayed = jnp.concatenate(
            [gathered[start : start + block], gathered[start + stride : start + stride + block]],
            axis=0,
        )
        summed = hidden[:, lanes] + matmul_nt(eye, relayed)
        hidden[:, lanes] = summed
        if p == 0:
            near = jnp.mean(summed, axis=1, keepdims=True)
        apart = summed - near
        total = total + jnp.sum(apart, axis=1, keepdims=True)
        squares = squares + jnp.sum(apart * apart, axis=1, keepdims=True)
    shift = total * (1.0 / model)
    mean = near + shift
    inverse = lax.rsqrt(squares * (1.0 / model) - shift * shift + 1e-06)
    for lanes in spans:
        scaled = ((hidden[:, lanes] - mean) * inverse) * (1.0 + modulation[1:2, lanes])
        normed[:, lanes] = (scaled + modulation[0:1, lanes]).astype(jnp.bfloat16)
    first = pl.multiple_of(me[0] * count, count)
    hidden_out[...] = hidden[pl.ds(first, count), :].astype(jnp.bfloat16)
    for j, weight in enumerate((q_weight, k_weight, v_weight)):
        columns[j * width : (j + 1) * width] = matmul_nt(weight[...], normed[...]).astype(
            jnp.bfloat16
        )


def attend_kernel(place, gathered, out, queries, keys, values):
    team, tall, rows = gathered.shape
    width = tall // 3
    teams, count, _ = out.shape
    for r in range(team):
        span = slice(r * width, (r + 1) * width)
        queries[span] = gathered[r, :width]
        keys[span] = gathered[r, width : 2 * width]
        values[span] = gathered[r, 2 * width :]
    line = lax.broadcasted_iota(jnp.int32, (teams * count, rows), 0)
    wanted = ((line // count) * team + place[0]) * count + line % count
    pick = (wanted == lax.broadcasted_iota(jnp.int32, (teams * count, rows), 1)).astype(
        jnp.bfloat16
    )
    chosen = matmul_nt(pick, queries[...]).astype(jnp.bfloat16)
    for h in range(team * width // HEAD_DIM):
        span = slice(h * HEAD_DIM, (h + 1) * HEAD_DIM)
        scores = jnp.dot(
            chosen[:, span], keys[span], preferred_element_type=jnp.float32
        ) / math.sqrt(HEAD_DIM)
        expo = jnp.exp(scores - jnp.max(scores, axis=1, keepdims=True))
        denom = jnp.sum(expo, axis=1, keepdims=True)
        mixed = matmul_nt(expo.astype(jnp.bfloat16), values[span]) / denom
        out[:, :, span] = mixed.reshape(teams, count, HEAD_DIM).astype(jnp.bfloat16)


def on_device(
    devices,
    control,
    mask_ids,
    owner,
    mask_table,
    res_weight,
    base,
    modulation,
    q_weight,
    k_weight,
    v_weight,
):
    count, model = base.shape
    rows = owner.shape[0]
    block = res_weight.shape[1]
    width = q_weight.shape[1]
    ring = ring_order(devices)
    team = math.lcm(width, HEAD_DIM) // width
    teams = devices // team
    me = lax.axis_index("seq")
    bf16 = jnp.bfloat16
    shape = jax.ShapeDtypeStruct

    tiles = ((GATHER_BYTES - 1) // (2 * devices * rows) - block) // count
    head = model - tiles * LANES

    inputs = (mask_ids, control, mask_table, base, owner.reshape(1, rows))
    mine, tail, near_owner = call(
        condition_kernel,
        (
            pltpu.VMEM((count, model + head), bf16),
            pltpu.VMEM((tiles * count, LANES), bf16),
            pltpu.VMEM((1, rows), jnp.int32),
        ),
        [HBM] * len(inputs),
        [
            pltpu.SMEM((count,), jnp.int32),
            pltpu.VMEM(mask_table.shape, bf16),
            pltpu.VMEM((count, model), bf16),
            pltpu.VMEM((count, model), bf16),
            pltpu.SemaphoreType.DMA((len(inputs),)),
        ],
    )(*[pltpu.with_memory_space_constraint(x, pltpu.HBM) for x in inputs])
    team_groups = [[t * team + r for r in range(team)] for t in range(teams)]
    sent = [
        lax.ppermute(mine, "seq", [(d, d ^ (k * team)) for d in range(devices)])
        for k in range(1, teams)
    ]
    own = lax.all_gather(mine, "seq", axis=0, tiled=True, axis_index_groups=team_groups)
    others = lax.all_gather(
        jnp.concatenate(sent, axis=0), "seq", axis=0, tiled=True, axis_index_groups=team_groups
    )
    payload = call(
        functools.partial(residual_kernel, team),
        shape((block + tiles * count, rows), bf16),
        [SMEM] + [VMEM] * 5,
        [pltpu.VMEM((rows, model), bf16)],
    )(me.reshape(1), own, others, res_weight.T, near_owner, tail)
    gathered = lax.all_gather(payload, "seq", axis=0, tiled=True, axis_index_groups=[ring])
    columns, hidden_out = call(
        functools.partial(project_kernel, ring, team),
        (shape((3 * width, rows), bf16), shape((count, model), bf16)),
        [SMEM] + [VMEM] * 7,
        [pltpu.VMEM((rows, model), jnp.float32), pltpu.VMEM((rows, model), bf16)],
    )(me.reshape(1), gathered, own, others, modulation, q_weight.T, k_weight.T, v_weight.T)
    columns = lax.all_gather(columns, "seq", axis=0, axis_index_groups=team_groups)
    head_columns = team * width
    mine = call(
        attend_kernel,
        shape((teams, count, head_columns), bf16),
        [SMEM, VMEM],
        [pltpu.VMEM((head_columns, rows), bf16)] * 3,
    )((me % team).reshape(1), columns)
    place_groups = [[t * team + r for t in range(teams)] for r in range(team)]
    parts = lax.all_to_all(
        mine, "seq", split_axis=0, concat_axis=0, tiled=True, axis_index_groups=place_groups
    )
    attended = parts.transpose(1, 0, 2).reshape(count, teams * head_columns)
    return (hidden_out, attended)


def fits(devices, rows, block, width):
    team = math.lcm(width, HEAD_DIM) // width
    powers = all(n & (n - 1) == 0 for n in (devices, team))
    return rows == LANES and devices > team > 1 and powers and block % 64 == 0 and width % 16 == 0


def on_any_device(devices, *arguments):
    owner, res_weight, q_weight = arguments[2], arguments[4], arguments[7]
    tidy = fits(devices, owner.shape[0], res_weight.shape[1], q_weight.shape[1])
    return (on_device if tidy else on_device_plain)(devices, *arguments)


def solution(mesh):
    in_specs = (
        P(("parts", "seq"), None),
        P(("parts", "seq")),
        P("parts"),
        P(),
        P(None, "seq"),
        P(("parts", "seq"), None),
        P(),
        P(None, "seq"),
        P(None, "seq"),
        P(None, "seq"),
    )
    out_specs = (P(("parts", "seq"), None), P(("parts", "seq"), None))
    return jax.shard_map(
        functools.partial(on_any_device, mesh.shape["seq"]),
        mesh=mesh,
        in_specs=in_specs,
        out_specs=out_specs,
        check_vma=False,
    )
```

```python
import functools
import math

import jax
import jax.numpy as jnp
from jax import lax
from jax.experimental import pallas as pl
from jax.experimental.pallas import tpu as pltpu
from jax.sharding import PartitionSpec as P


HEAD_DIM = 128


def ring_order(devices):
    chips = devices // 2
    narrow = 1
    while (2 * narrow) ** 2 <= chips and chips % (2 * narrow) == 0:
        narrow *= 2
    long = chips // narrow
    if narrow == 1:
        walk = [(row, 0) for row in range(long)]
    else:
        walk = [(row, 0) for row in range(long)]
        for back, row in enumerate(reversed(range(long))):
            columns = range(1, narrow) if back % 2 == 0 else range(narrow - 1, 0, -1)
            walk += [(row, column) for column in columns]
    return [(row * narrow + column) * 2 + core for row, column in walk for core in range(2)]


def layer_norm(hidden, modulation):
    row_mean = jnp.mean(hidden, axis=1, keepdims=True)
    centred = hidden - row_mean
    row_var = jnp.mean(centred * centred, axis=1, keepdims=True)
    scaled = centred * lax.rsqrt(row_var + 1e-06)
    return (scaled * (1.0 + modulation[1]) + modulation[0]).astype(jnp.bfloat16)


def on_device_plain(
    devices,
    control,
    mask_ids,
    owner,
    mask_table,
    res_weight,
    base,
    modulation,
    q_weight,
    k_weight,
    v_weight,
):
    row_count = base.shape[0]
    total_rows = owner.shape[0]
    width = q_weight.shape[1]
    ring = ring_order(devices)
    team = math.lcm(width, HEAD_DIM) // width
    teams = devices // team
    team_heads = team * width // HEAD_DIM
    me = lax.axis_index("seq")
    place = me % team

    selector = (
        mask_ids[:, None] == jnp.arange(mask_table.shape[0], dtype=jnp.int32)[None, :]
    ).astype(jnp.bfloat16)
    condition = (
        control.astype(jnp.float32)
        + jnp.dot(selector, mask_table, preferred_element_type=jnp.float32)
    ).astype(jnp.bfloat16)
    conditions = lax.all_gather(condition, "seq", axis=0, tiled=True, axis_index_groups=[ring])
    residual = jnp.dot(conditions, res_weight, preferred_element_type=jnp.float32).astype(
        jnp.bfloat16
    )
    owner_ring = jnp.concatenate(
        [owner[place_ * row_count : (place_ + 1) * row_count] for place_ in ring]
    )
    relay = (jnp.arange(total_rows, dtype=jnp.int32)[:, None] == owner_ring[None, :]).astype(
        jnp.bfloat16
    )
    by_owner = jnp.dot(relay, residual, preferred_element_type=jnp.float32).astype(jnp.bfloat16)
    relayed = lax.all_to_all(by_owner, "seq", split_axis=0, concat_axis=1, tiled=True)
    hidden = base.astype(jnp.float32) + relayed.astype(jnp.float32)
    normed = layer_norm(hidden, modulation)
    joined = jnp.concatenate([q_weight, k_weight, v_weight], axis=1)
    normed_all = lax.all_gather(normed, "seq", axis=0, tiled=True, axis_index_groups=[ring])
    columns = lax.dot_general(
        joined, normed_all, (((0,), (1,)), ((), ())), preferred_element_type=jnp.float32
    ).astype(jnp.bfloat16)
    team_groups = [[t * team + r for r in range(team)] for t in range(teams)]
    columns = lax.all_gather(columns, "seq", axis=0, axis_index_groups=team_groups)
    columns = columns.reshape(team, 3, width, total_rows).transpose(1, 0, 2, 3)
    columns = columns.reshape(3, team_heads, HEAD_DIM, total_rows)
    spots = jnp.array([ring.index(d) for d in range(devices)], jnp.int32).reshape(teams, team)
    blocks = columns[0].reshape(team_heads, HEAD_DIM, devices, row_count)
    queries = jnp.take(blocks, jnp.take(spots, place, axis=1), axis=2)
    queries = queries.reshape(team_heads, HEAD_DIM, teams * row_count)
    scores = jnp.einsum(
        "hdt,hdk->htk", queries, columns[1], preferred_element_type=jnp.float32
    ) / math.sqrt(HEAD_DIM)
    expo = jnp.exp(scores - jnp.max(scores, axis=2, keepdims=True))
    denom = jnp.sum(expo, axis=2)
    summed = jnp.einsum(
        "htk,hdk->thd",
        expo.astype(jnp.bfloat16),
        columns[2],
        preferred_element_type=jnp.float32,
    )
    mine = (summed / denom.T[:, :, None]).astype(jnp.bfloat16)
    mine = mine.reshape(teams, row_count, team_heads * HEAD_DIM)
    place_groups = [[t * team + r for t in range(teams)] for r in range(team)]
    parts = lax.all_to_all(
        mine, "seq", split_axis=0, concat_axis=0, tiled=True, axis_index_groups=place_groups
    )
    attended = parts.transpose(1, 0, 2).reshape(row_count, teams * team_heads * HEAD_DIM)
    return (hidden.astype(jnp.bfloat16), attended)


VMEM = pl.BlockSpec(memory_space=pltpu.VMEM)
SMEM = pl.BlockSpec(memory_space=pltpu.SMEM)
HBM = pl.BlockSpec(memory_space=pltpu.HBM)
NT = (((1,), (1,)), ((), ()))
LANES = 128
GATHER_BYTES = 1 << 20


def call(kernel, out_shape, in_specs, scratch=(), limit=8 << 20):
    multiple = isinstance(out_shape, (tuple, list))
    return pl.pallas_call(
        kernel,
        out_shape=out_shape,
        in_specs=in_specs,
        out_specs=[VMEM] * len(out_shape) if multiple else VMEM,
        scratch_shapes=list(scratch),
        compiler_params=pltpu.CompilerParams(vmem_limit_bytes=limit),
    )


def matmul_nt(left, right):
    return lax.dot_general(left, right, NT, preferred_element_type=jnp.float32)


def identity(size):
    rows = lax.broadcasted_iota(jnp.int32, (size, size), 0)
    return (rows == lax.broadcasted_iota(jnp.int32, (size, size), 1)).astype(jnp.bfloat16)


def condition_kernel(
    far_ids,
    far_control,
    far_table,
    far_base,
    far_owner,
    block,
    tail,
    owner,
    ids,
    table,
    control,
    base,
    arrived,
):
    copies = [
        pltpu.make_async_copy(source, target, arrived.at[i])
        for i, (source, target) in enumerate(
            (
                (far_ids, ids),
                (far_table, table),
                (far_control, control),
                (far_base, base),
                (far_owner, owner),
            )
        )
    ]
    for copy in copies:
        copy.start()
    rows, model = control.shape
    kinds = table.shape[0]
    head = block.shape[1] - model
    copies[0].wait()
    kind = jnp.zeros((rows, 1), jnp.int32)
    row = lax.broadcasted_iota(jnp.int32, (rows, 1), 0)
    for i in range(rows):
        kind = jnp.where(row == i, ids[i], kind)
    copies[1].wait()
    copies[2].wait()
    entries = table[...].astype(jnp.float32)
    chosen = jnp.broadcast_to(entries[:1], (rows, model))
    for j in range(1, kinds):
        chosen = jnp.where(kind == j, entries[j : j + 1], chosen)
    block[:, :model] = (control[...].astype(jnp.float32) + chosen).astype(jnp.bfloat16)
    copies[3].wait()
    block[:, model:] = base[:, :head]
    for tile in range(tail.shape[0] // rows):
        lanes = slice(head + tile * LANES, head + (tile + 1) * LANES)
        tail[tile * rows : (tile + 1) * rows] = base[:, lanes]
    copies[4].wait()


def natural_rows(me, team, near, rows):
    count = near // team
    far = (rows - near) // near
    lane = lax.broadcasted_iota(jnp.int32, (1, rows), 1)
    block_at = lane // count
    beyond = block_at - team
    step = jnp.where(beyond < 0, 0, beyond % far + 1)
    member = jnp.where(beyond < 0, block_at, beyond // far)
    holder = ((me // team) ^ step) * team + member
    row = lax.broadcasted_iota(jnp.int32, (rows, rows), 0)
    return (row == holder * count + lane % count).astype(jnp.bfloat16)


def residual_kernel(team, me, own, others, weight, owner, tail, out):
    block, model = weight.shape
    near = own.shape[0]
    rows = near + others.shape[0]
    conditions = jnp.concatenate([own[:, :model], others[:, :model]], axis=0)
    residual = matmul_nt(weight[...], conditions).astype(jnp.bfloat16)
    row = lax.broadcasted_iota(jnp.int32, (rows, rows), 0)
    names = (row == owner[...]).astype(jnp.bfloat16)
    relay = jnp.dot(
        names, natural_rows(me[0], team, near, rows), preferred_element_type=jnp.float32
    ).astype(jnp.bfloat16)
    out[:block] = matmul_nt(residual, relay).astype(jnp.bfloat16)
    out[block:] = tail[...]


def fold(values):
    tiles = [values[:, i : i + LANES] for i in range(0, values.shape[1], LANES)]
    return sum(tiles[1:], tiles[0])


def project_kernel(
    ring,
    team,
    me,
    gathered,
    own,
    others,
    modulation,
    q_weight,
    k_weight,
    v_weight,
    columns,
    hidden_out,
    hidden,
    normed,
):
    devices = len(ring)
    rows, model = hidden.shape
    stride = gathered.shape[0] // devices
    block = model // devices
    count = hidden_out.shape[0]
    head = own.shape[1] - model
    turned = natural_rows(me[0], team, own.shape[0], rows)
    eye = identity(rows)
    pair = 2 * block
    spans = []
    total = jnp.zeros((rows, LANES), jnp.float32)
    squares = jnp.zeros((rows, LANES), jnp.float32)
    for p in range(devices // 2):
        first = ring[2 * p] * block
        lanes = slice(first, first + pair)
        spans.append(lanes)
        start = 2 * p * stride
        relayed = jnp.concatenate(
            [gathered[start : start + block], gathered[start + stride : start + stride + block]],
            axis=0,
        )
        if first < head:
            there = slice(model + first, model + first + pair)
            placed = jnp.dot(
                turned,
                jnp.concatenate([own[:, there], others[:, there]], axis=0),
                preferred_element_type=jnp.float32,
            )
        else:
            for tile in range(pair // LANES):
                at = first + tile * LANES
                for s, device in enumerate(ring):
                    row = s * stride + block + (at - head) // LANES * count
                    hidden[device * count : (device + 1) * count, at : at + LANES] = gathered[
                        row : row + count
                    ].astype(jnp.float32)
            placed = hidden[:, lanes]
        summed = placed + matmul_nt(eye, relayed)
        hidden[:, lanes] = summed
        if p == 0:
            near = jnp.sum(fold(summed), axis=1, keepdims=True) * (1.0 / pair)
        apart = summed - near
        total = total + fold(apart)
        squares = squares + fold(apart * apart)
    shift = jnp.sum(total, axis=1, keepdims=True) * (1.0 / model)
    mean = near + shift
    spread = jnp.sum(squares, axis=1, keepdims=True) * (1.0 / model) - shift * shift
    inverse = lax.rsqrt(spread + 1e-06)
    for lanes in spans:
        scaled = ((hidden[:, lanes] - mean) * inverse) * (1.0 + modulation[1:2, lanes])
        normed[:, lanes] = (scaled + modulation[0:1, lanes]).astype(jnp.bfloat16)
    first = pl.multiple_of(me[0] * count, count)
    hidden_out[...] = hidden[pl.ds(first, count), :].astype(jnp.bfloat16)
    weights = jnp.concatenate([q_weight[...], k_weight[...], v_weight[...]], axis=0)
    columns[...] = matmul_nt(weights, normed[...]).astype(jnp.bfloat16)


def attend_kernel(me, gathered, *refs):
    outs, (queries, keys, values) = refs[:-3], refs[-3:]
    team, tall, rows = gathered.shape
    width = tall // 3
    teams, count = len(outs), outs[0].shape[0]
    for r in range(team):
        span = slice(r * width, (r + 1) * width)
        queries[span] = gathered[r, :width]
        keys[span] = gathered[r, width : 2 * width]
        values[span] = gathered[r, 2 * width :]
    line = lax.broadcasted_iota(jnp.int32, (teams * count, rows), 0)
    wanted = (((me[0] // team) ^ (line // count)) * team + me[0] % team) * count + line % count
    pick = (wanted == lax.broadcasted_iota(jnp.int32, (teams * count, rows), 1)).astype(
        jnp.bfloat16
    )
    chosen = matmul_nt(pick, queries[...]).astype(jnp.bfloat16)
    for h in range(team * width // HEAD_DIM):
        span = slice(h * HEAD_DIM, (h + 1) * HEAD_DIM)
        scores = jnp.dot(
            chosen[:, span], keys[span], preferred_element_type=jnp.float32
        ) / math.sqrt(HEAD_DIM)
        expo = jnp.exp(scores - jnp.max(scores, axis=1, keepdims=True))
        denom = jnp.sum(expo, axis=1, keepdims=True)
        mixed = matmul_nt(expo.astype(jnp.bfloat16), values[span]) / denom
        for k, out in enumerate(outs):
            out[:, span] = mixed[k * count : (k + 1) * count].astype(jnp.bfloat16)


def gather_kernel(team, me, *refs):
    blocks, out = refs[:-1], refs[-1]
    columns = blocks[0].shape[1]
    for k, block in enumerate(blocks):
        first = pl.multiple_of(((me[0] // team) ^ k) * columns, columns)
        out[:, pl.ds(first, columns)] = block[...]


def on_device(
    devices,
    control,
    mask_ids,
    owner,
    mask_table,
    res_weight,
    base,
    modulation,
    q_weight,
    k_weight,
    v_weight,
):
    count, model = base.shape
    rows = owner.shape[0]
    block = res_weight.shape[1]
    width = q_weight.shape[1]
    ring = ring_order(devices)
    team = math.lcm(width, HEAD_DIM) // width
    teams = devices // team
    me = lax.axis_index("seq")
    bf16 = jnp.bfloat16
    shape = jax.ShapeDtypeStruct

    tiles = ((GATHER_BYTES - 1) // (2 * devices * rows) - block) // count
    tiles -= tiles % (2 * block // LANES)
    head = model - tiles * LANES

    inputs = (mask_ids, control, mask_table, base, owner.reshape(1, rows))
    mine, tail, near_owner = call(
        condition_kernel,
        (
            pltpu.VMEM((count, model + head), bf16),
            pltpu.VMEM((tiles * count, LANES), bf16),
            pltpu.VMEM((1, rows), jnp.int32),
        ),
        [HBM] * len(inputs),
        [
            pltpu.SMEM((count,), jnp.int32),
            pltpu.VMEM(mask_table.shape, bf16),
            pltpu.VMEM((count, model), bf16),
            pltpu.VMEM((count, model), bf16),
            pltpu.SemaphoreType.DMA((len(inputs),)),
        ],
    )(*[pltpu.with_memory_space_constraint(x, pltpu.HBM) for x in inputs])
    team_groups = [[t * team + r for r in range(team)] for t in range(teams)]
    sent = [
        lax.ppermute(mine, "seq", [(d, d ^ (k * team)) for d in range(devices)])
        for k in range(1, teams)
    ]
    own = lax.all_gather(mine, "seq", axis=0, tiled=True, axis_index_groups=team_groups)
    others = lax.all_gather(
        jnp.concatenate(sent, axis=0), "seq", axis=0, tiled=True, axis_index_groups=team_groups
    )
    payload = call(
        functools.partial(residual_kernel, team),
        shape((block + tiles * count, rows), bf16),
        [SMEM] + [VMEM] * 5,
    )(me.reshape(1), own, others, res_weight.T, near_owner, tail)
    gathered = lax.all_gather(payload, "seq", axis=0, tiled=True, axis_index_groups=[ring])
    columns, hidden_out = call(
        functools.partial(project_kernel, ring, team),
        (shape((3 * width, rows), bf16), shape((count, model), bf16)),
        [SMEM] + [VMEM] * 7,
        [pltpu.VMEM((rows, model), jnp.float32), pltpu.VMEM((rows, model), bf16)],
    )(me.reshape(1), gathered, own, others, modulation, q_weight.T, k_weight.T, v_weight.T)
    columns = lax.all_gather(columns, "seq", axis=0, axis_index_groups=team_groups)
    head_columns = team * width
    results = call(
        attend_kernel,
        tuple(shape((count, head_columns), bf16) for _ in range(teams)),
        [SMEM, VMEM],
        [pltpu.VMEM((head_columns, rows), bf16)] * 3,
    )(me.reshape(1), columns)
    crossed = {}
    for k in range(1, teams):
        crossed[k] = lax.ppermute(results[k], "seq", [(d, d ^ (k * team)) for d in range(devices)])
    parts = [results[0]] + [crossed[k] for k in range(1, teams)]
    attended = call(
        functools.partial(gather_kernel, team),
        shape((count, teams * head_columns), bf16),
        [SMEM] + [VMEM] * teams,
    )(me.reshape(1), *parts)
    return (hidden_out, attended)


def fits(devices, rows, block, width):
    team = math.lcm(width, HEAD_DIM) // width
    powers = all(n & (n - 1) == 0 for n in (devices, team))
    return rows == LANES and devices > team > 1 and powers and block % 64 == 0 and width % 16 == 0


def on_any_device(devices, *arguments):
    owner, res_weight, q_weight = arguments[2], arguments[4], arguments[7]
    tidy = fits(devices, owner.shape[0], res_weight.shape[1], q_weight.shape[1])
    return (on_device if tidy else on_device_plain)(devices, *arguments)


def solution(mesh):
    in_specs = (
        P(("parts", "seq"), None),
        P(("parts", "seq")),
        P("parts"),
        P(),
        P(None, "seq"),
        P(("parts", "seq"), None),
        P(),
        P(None, "seq"),
        P(None, "seq"),
        P(None, "seq"),
    )
    out_specs = (P(("parts", "seq"), None), P(("parts", "seq"), None))
    return jax.shard_map(
        functools.partial(on_any_device, mesh.shape["seq"]),
        mesh=mesh,
        in_specs=in_specs,
        out_specs=out_specs,
        check_vma=False,
    )
```

```python
import functools
import math

import jax
import jax.numpy as jnp
from jax import lax
from jax.experimental import pallas as pl
from jax.experimental.pallas import tpu as pltpu
from jax.sharding import PartitionSpec as P


HEAD_DIM = 128


def ring_order(devices):
    chips = devices // 2
    narrow = 1
    while (2 * narrow) ** 2 <= chips and chips % (2 * narrow) == 0:
        narrow *= 2
    long = chips // narrow
    if narrow == 1:
        walk = [(row, 0) for row in range(long)]
    else:
        walk = [(row, 0) for row in range(long)]
        for back, row in enumerate(reversed(range(long))):
            columns = range(1, narrow) if back % 2 == 0 else range(narrow - 1, 0, -1)
            walk += [(row, column) for column in columns]
    return [(row * narrow + column) * 2 + core for row, column in walk for core in range(2)]


def layer_norm(hidden, modulation):
    row_mean = jnp.mean(hidden, axis=1, keepdims=True)
    centred = hidden - row_mean
    row_var = jnp.mean(centred * centred, axis=1, keepdims=True)
    scaled = centred * lax.rsqrt(row_var + 1e-06)
    return (scaled * (1.0 + modulation[1]) + modulation[0]).astype(jnp.bfloat16)


def on_device_plain(
    devices,
    control,
    mask_ids,
    owner,
    mask_table,
    res_weight,
    base,
    modulation,
    q_weight,
    k_weight,
    v_weight,
):
    row_count = base.shape[0]
    total_rows = owner.shape[0]
    width = q_weight.shape[1]
    ring = ring_order(devices)
    team = math.lcm(width, HEAD_DIM) // width
    teams = devices // team
    team_heads = team * width // HEAD_DIM
    me = lax.axis_index("seq")
    place = me % team

    selector = (
        mask_ids[:, None] == jnp.arange(mask_table.shape[0], dtype=jnp.int32)[None, :]
    ).astype(jnp.bfloat16)
    condition = (
        control.astype(jnp.float32)
        + jnp.dot(selector, mask_table, preferred_element_type=jnp.float32)
    ).astype(jnp.bfloat16)
    conditions = lax.all_gather(condition, "seq", axis=0, tiled=True, axis_index_groups=[ring])
    residual = jnp.dot(conditions, res_weight, preferred_element_type=jnp.float32).astype(
        jnp.bfloat16
    )
    owner_ring = jnp.concatenate(
        [owner[place_ * row_count : (place_ + 1) * row_count] for place_ in ring]
    )
    relay = (jnp.arange(total_rows, dtype=jnp.int32)[:, None] == owner_ring[None, :]).astype(
        jnp.bfloat16
    )
    by_owner = jnp.dot(relay, residual, preferred_element_type=jnp.float32).astype(jnp.bfloat16)
    relayed = lax.all_to_all(by_owner, "seq", split_axis=0, concat_axis=1, tiled=True)
    hidden = base.astype(jnp.float32) + relayed.astype(jnp.float32)
    normed = layer_norm(hidden, modulation)
    joined = jnp.concatenate([q_weight, k_weight, v_weight], axis=1)
    normed_all = lax.all_gather(normed, "seq", axis=0, tiled=True, axis_index_groups=[ring])
    columns = lax.dot_general(
        joined, normed_all, (((0,), (1,)), ((), ())), preferred_element_type=jnp.float32
    ).astype(jnp.bfloat16)
    team_groups = [[t * team + r for r in range(team)] for t in range(teams)]
    columns = lax.all_gather(columns, "seq", axis=0, axis_index_groups=team_groups)
    columns = columns.reshape(team, 3, width, total_rows).transpose(1, 0, 2, 3)
    columns = columns.reshape(3, team_heads, HEAD_DIM, total_rows)
    spots = jnp.array([ring.index(d) for d in range(devices)], jnp.int32).reshape(teams, team)
    blocks = columns[0].reshape(team_heads, HEAD_DIM, devices, row_count)
    queries = jnp.take(blocks, jnp.take(spots, place, axis=1), axis=2)
    queries = queries.reshape(team_heads, HEAD_DIM, teams * row_count)
    scores = jnp.einsum(
        "hdt,hdk->htk", queries, columns[1], preferred_element_type=jnp.float32
    ) / math.sqrt(HEAD_DIM)
    expo = jnp.exp(scores - jnp.max(scores, axis=2, keepdims=True))
    denom = jnp.sum(expo, axis=2)
    summed = jnp.einsum(
        "htk,hdk->thd",
        expo.astype(jnp.bfloat16),
        columns[2],
        preferred_element_type=jnp.float32,
    )
    mine = (summed / denom.T[:, :, None]).astype(jnp.bfloat16)
    mine = mine.reshape(teams, row_count, team_heads * HEAD_DIM)
    place_groups = [[t * team + r for t in range(teams)] for r in range(team)]
    parts = lax.all_to_all(
        mine, "seq", split_axis=0, concat_axis=0, tiled=True, axis_index_groups=place_groups
    )
    attended = parts.transpose(1, 0, 2).reshape(row_count, teams * team_heads * HEAD_DIM)
    return (hidden.astype(jnp.bfloat16), attended)


VMEM = pl.BlockSpec(memory_space=pltpu.VMEM)
SMEM = pl.BlockSpec(memory_space=pltpu.SMEM)
HBM = pl.BlockSpec(memory_space=pltpu.HBM)
NT = (((1,), (1,)), ((), ()))
LANES = 128
GATHER_BYTES = 1 << 20


def call(kernel, out_shape, in_specs, scratch=(), limit=8 << 20):
    multiple = isinstance(out_shape, (tuple, list))
    return pl.pallas_call(
        kernel,
        out_shape=out_shape,
        in_specs=in_specs,
        out_specs=[VMEM] * len(out_shape) if multiple else VMEM,
        scratch_shapes=list(scratch),
        compiler_params=pltpu.CompilerParams(vmem_limit_bytes=limit),
    )


def matmul_nt(left, right):
    return lax.dot_general(left, right, NT, preferred_element_type=jnp.float32)


def identity(size):
    rows = lax.broadcasted_iota(jnp.int32, (size, size), 0)
    return (rows == lax.broadcasted_iota(jnp.int32, (size, size), 1)).astype(jnp.bfloat16)


def condition_kernel(
    far_ids,
    far_control,
    far_table,
    far_base,
    far_owner,
    block,
    tail,
    owner,
    ids,
    table,
    control,
    base,
    arrived,
):
    copies = [
        pltpu.make_async_copy(source, target, arrived.at[i])
        for i, (source, target) in enumerate(
            (
                (far_ids, ids),
                (far_table, table),
                (far_control, control),
                (far_base, base),
                (far_owner, owner),
            )
        )
    ]
    for copy in copies:
        copy.start()
    rows, model = control.shape
    kinds = table.shape[0]
    head = block.shape[1] - model
    copies[0].wait()
    kind = jnp.zeros((rows, 1), jnp.int32)
    row = lax.broadcasted_iota(jnp.int32, (rows, 1), 0)
    for i in range(rows):
        kind = jnp.where(row == i, ids[i], kind)
    copies[1].wait()
    copies[2].wait()
    entries = table[...].astype(jnp.float32)
    chosen = jnp.broadcast_to(entries[:1], (rows, model))
    for j in range(1, kinds):
        chosen = jnp.where(kind == j, entries[j : j + 1], chosen)
    block[:, :model] = (control[...].astype(jnp.float32) + chosen).astype(jnp.bfloat16)
    copies[3].wait()
    block[:, model:] = base[:, :head]
    for tile in range(tail.shape[0] // rows):
        lanes = slice(head + tile * LANES, head + (tile + 1) * LANES)
        tail[tile * rows : (tile + 1) * rows] = base[:, lanes]
    copies[4].wait()


def natural_rows(me, team, count, rows):
    far = rows // (team * count) - 1
    lane = lax.broadcasted_iota(jnp.int32, (1, rows), 1)
    block_at = lane // count
    beyond = block_at - team
    step = jnp.where(beyond < 0, 0, beyond % far + 1)
    member = jnp.where(beyond < 0, block_at ^ (me % team), beyond // far)
    holder = ((me // team) ^ step) * team + member
    row = lax.broadcasted_iota(jnp.int32, (rows, rows), 0)
    return (row == holder * count + lane % count).astype(jnp.bfloat16)


def stack(blocks, columns):
    return jnp.concatenate([block[:, columns] for block in blocks], axis=0)


def residual_kernel(team, me, *refs):
    blocks, (weight, owner, tail, out) = refs[:-4], refs[-4:]
    block, model = weight.shape
    rows = owner.shape[1]
    conditions = stack(blocks, slice(model))
    residual = matmul_nt(weight[...], conditions).astype(jnp.bfloat16)
    row = lax.broadcasted_iota(jnp.int32, (rows, rows), 0)
    names = (row == owner[...]).astype(jnp.bfloat16)
    relay = jnp.dot(
        names,
        natural_rows(me[0], team, blocks[0].shape[0], rows),
        preferred_element_type=jnp.float32,
    ).astype(jnp.bfloat16)
    out[:block] = matmul_nt(residual, relay).astype(jnp.bfloat16)
    out[block:] = tail[...]


def fold(values):
    tiles = [values[:, i : i + LANES] for i in range(0, values.shape[1], LANES)]
    return sum(tiles[1:], tiles[0])


def project_kernel(
    ring,
    team,
    me,
    gathered,
    *refs,
):
    blocks = refs[: team + 1]
    modulation, q_weight, k_weight, v_weight = refs[team + 1 : team + 5]
    columns, hidden_out, hidden, normed = refs[team + 5 :]
    devices = len(ring)
    rows, model = hidden.shape
    stride = gathered.shape[0] // devices
    block = model // devices
    count = hidden_out.shape[0]
    head = blocks[0].shape[1] - model
    turned = natural_rows(me[0], team, count, rows)
    eye = identity(rows)
    pair = 2 * block
    spans = []
    total = jnp.zeros((rows, LANES), jnp.float32)
    squares = jnp.zeros((rows, LANES), jnp.float32)
    for p in range(devices // 2):
        first = ring[2 * p] * block
        lanes = slice(first, first + pair)
        spans.append(lanes)
        start = 2 * p * stride
        relayed = jnp.concatenate(
            [gathered[start : start + block], gathered[start + stride : start + stride + block]],
            axis=0,
        )
        if first < head:
            there = slice(model + first, model + first + pair)
            placed = jnp.dot(
                turned,
                stack(blocks, there),
                preferred_element_type=jnp.float32,
            )
        else:
            for tile in range(pair // LANES):
                at = first + tile * LANES
                for s, device in enumerate(ring):
                    row = s * stride + block + (at - head) // LANES * count
                    hidden[device * count : (device + 1) * count, at : at + LANES] = gathered[
                        row : row + count
                    ].astype(jnp.float32)
            placed = hidden[:, lanes]
        summed = placed + matmul_nt(eye, relayed)
        hidden[:, lanes] = summed
        if p == 0:
            near = jnp.sum(fold(summed), axis=1, keepdims=True) * (1.0 / pair)
        apart = summed - near
        total = total + fold(apart)
        squares = squares + fold(apart * apart)
    shift = jnp.sum(total, axis=1, keepdims=True) * (1.0 / model)
    mean = near + shift
    spread = jnp.sum(squares, axis=1, keepdims=True) * (1.0 / model) - shift * shift
    inverse = lax.rsqrt(spread + 1e-06)
    for lanes in spans:
        scaled = ((hidden[:, lanes] - mean) * inverse) * (1.0 + modulation[1:2, lanes])
        normed[:, lanes] = (scaled + modulation[0:1, lanes]).astype(jnp.bfloat16)
    first = pl.multiple_of(me[0] * count, count)
    hidden_out[...] = hidden[pl.ds(first, count), :].astype(jnp.bfloat16)
    weights = jnp.concatenate([q_weight[...], k_weight[...], v_weight[...]], axis=0)
    columns[...] = matmul_nt(weights, normed[...]).astype(jnp.bfloat16)


def attend_kernel(me, gathered, *refs):
    outs, (queries, keys, values) = refs[:-3], refs[-3:]
    team, tall, rows = gathered.shape
    width = tall // 3
    teams, count = len(outs), outs[0].shape[0]
    for r in range(team):
        span = slice(r * width, (r + 1) * width)
        queries[span] = gathered[r, :width]
        keys[span] = gathered[r, width : 2 * width]
        values[span] = gathered[r, 2 * width :]
    line = lax.broadcasted_iota(jnp.int32, (teams * count, rows), 0)
    wanted = (((me[0] // team) ^ (line // count)) * team + me[0] % team) * count + line % count
    pick = (wanted == lax.broadcasted_iota(jnp.int32, (teams * count, rows), 1)).astype(
        jnp.bfloat16
    )
    chosen = matmul_nt(pick, queries[...]).astype(jnp.bfloat16)
    for h in range(team * width // HEAD_DIM):
        span = slice(h * HEAD_DIM, (h + 1) * HEAD_DIM)
        scores = jnp.dot(
            chosen[:, span], keys[span], preferred_element_type=jnp.float32
        ) / math.sqrt(HEAD_DIM)
        expo = jnp.exp(scores - jnp.max(scores, axis=1, keepdims=True))
        denom = jnp.sum(expo, axis=1, keepdims=True)
        mixed = matmul_nt(expo.astype(jnp.bfloat16), values[span]) / denom
        for k, out in enumerate(outs):
            out[:, span] = mixed[k * count : (k + 1) * count].astype(jnp.bfloat16)


def gather_kernel(team, me, *refs):
    blocks, out = refs[:-1], refs[-1]
    columns = blocks[0].shape[1]
    for k, block in enumerate(blocks):
        first = pl.multiple_of(((me[0] // team) ^ k) * columns, columns)
        out[:, pl.ds(first, columns)] = block[...]


def exchange(values, devices, step):
    return lax.ppermute(values, "seq", [(d, d ^ step) for d in range(devices)])


def on_device(
    devices,
    control,
    mask_ids,
    owner,
    mask_table,
    res_weight,
    base,
    modulation,
    q_weight,
    k_weight,
    v_weight,
):
    count, model = base.shape
    rows = owner.shape[0]
    block = res_weight.shape[1]
    width = q_weight.shape[1]
    ring = ring_order(devices)
    team = math.lcm(width, HEAD_DIM) // width
    teams = devices // team
    me = lax.axis_index("seq")
    bf16 = jnp.bfloat16
    shape = jax.ShapeDtypeStruct

    tiles = ((GATHER_BYTES - 1) // (2 * devices * rows) - block) // count
    tiles -= tiles % (2 * block // LANES)
    head = model - tiles * LANES

    inputs = (mask_ids, control, mask_table, base, owner.reshape(1, rows))
    mine, tail, near_owner = call(
        condition_kernel,
        (
            pltpu.VMEM((count, model + head), bf16),
            pltpu.VMEM((tiles * count, LANES), bf16),
            pltpu.VMEM((1, rows), jnp.int32),
        ),
        [HBM] * len(inputs),
        [
            pltpu.SMEM((count,), jnp.int32),
            pltpu.VMEM(mask_table.shape, bf16),
            pltpu.VMEM((count, model), bf16),
            pltpu.VMEM((count, model), bf16),
            pltpu.SemaphoreType.DMA((len(inputs),)),
        ],
    )(*[pltpu.with_memory_space_constraint(x, pltpu.HBM) for x in inputs])
    team_groups = [[t * team + r for r in range(team)] for t in range(teams)]
    sent, near = [], [mine]
    for k in range(1, teams):
        sent.append(exchange(mine, devices, k * team))
    for k in range(1, team):
        near.append(exchange(mine, devices, k))
    others = lax.all_gather(
        jnp.concatenate(sent, axis=0), "seq", axis=0, tiled=True, axis_index_groups=team_groups
    )
    blocks = near + [others]
    payload = call(
        functools.partial(residual_kernel, team),
        shape((block + tiles * count, rows), bf16),
        [SMEM] + [VMEM] * (len(blocks) + 3),
    )(me.reshape(1), *blocks, res_weight.T, near_owner, tail)
    gathered = lax.all_gather(payload, "seq", axis=0, tiled=True, axis_index_groups=[ring])
    columns, hidden_out = call(
        functools.partial(project_kernel, ring, team),
        (shape((3 * width, rows), bf16), shape((count, model), bf16)),
        [SMEM] + [VMEM] * (len(blocks) + 5),
        [pltpu.VMEM((rows, model), jnp.float32), pltpu.VMEM((rows, model), bf16)],
    )(me.reshape(1), gathered, *blocks, modulation, q_weight.T, k_weight.T, v_weight.T)
    columns = lax.all_gather(columns, "seq", axis=0, axis_index_groups=team_groups)
    head_columns = team * width
    results = call(
        attend_kernel,
        tuple(shape((count, head_columns), bf16) for _ in range(teams)),
        [SMEM, VMEM],
        [pltpu.VMEM((head_columns, rows), bf16)] * 3,
    )(me.reshape(1), columns)
    crossed = {}
    for k in range(1, teams):
        crossed[k] = exchange(results[k], devices, k * team)
    parts = [results[0]] + [crossed[k] for k in range(1, teams)]
    attended = call(
        functools.partial(gather_kernel, team),
        shape((count, teams * head_columns), bf16),
        [SMEM] + [VMEM] * teams,
    )(me.reshape(1), *parts)
    return (hidden_out, attended)


def fits(devices, rows, block, width):
    team = math.lcm(width, HEAD_DIM) // width
    powers = all(n & (n - 1) == 0 for n in (devices, team))
    return rows == LANES and devices > team > 1 and powers and block % 64 == 0 and width % 16 == 0


def on_any_device(devices, *arguments):
    owner, res_weight, q_weight = arguments[2], arguments[4], arguments[7]
    tidy = fits(devices, owner.shape[0], res_weight.shape[1], q_weight.shape[1])
    return (on_device if tidy else on_device_plain)(devices, *arguments)


def solution(mesh):
    in_specs = (
        P(("parts", "seq"), None),
        P(("parts", "seq")),
        P("parts"),
        P(),
        P(None, "seq"),
        P(("parts", "seq"), None),
        P(),
        P(None, "seq"),
        P(None, "seq"),
        P(None, "seq"),
    )
    out_specs = (P(("parts", "seq"), None), P(("parts", "seq"), None))
    return jax.shard_map(
        functools.partial(on_any_device, mesh.shape["seq"]),
        mesh=mesh,
        in_specs=in_specs,
        out_specs=out_specs,
        check_vma=False,
    )
```

```python
import functools
import math

import jax
import jax.numpy as jnp
from jax import lax
from jax.experimental import pallas as pl
from jax.experimental.pallas import tpu as pltpu
from jax.sharding import PartitionSpec as P


HEAD_DIM = 128


def ring_order(devices):
    chips = devices // 2
    narrow = 1
    while (2 * narrow) ** 2 <= chips and chips % (2 * narrow) == 0:
        narrow *= 2
    long = chips // narrow
    if narrow == 1:
        walk = [(row, 0) for row in range(long)]
    else:
        walk = [(row, 0) for row in range(long)]
        for back, row in enumerate(reversed(range(long))):
            columns = range(1, narrow) if back % 2 == 0 else range(narrow - 1, 0, -1)
            walk += [(row, column) for column in columns]
    return [(row * narrow + column) * 2 + core for row, column in walk for core in range(2)]


def layer_norm(hidden, modulation):
    row_mean = jnp.mean(hidden, axis=1, keepdims=True)
    centred = hidden - row_mean
    row_var = jnp.mean(centred * centred, axis=1, keepdims=True)
    scaled = centred * lax.rsqrt(row_var + 1e-06)
    return (scaled * (1.0 + modulation[1]) + modulation[0]).astype(jnp.bfloat16)


def on_device_plain(
    devices,
    control,
    mask_ids,
    owner,
    mask_table,
    res_weight,
    base,
    modulation,
    q_weight,
    k_weight,
    v_weight,
):
    row_count = base.shape[0]
    total_rows = owner.shape[0]
    width = q_weight.shape[1]
    ring = ring_order(devices)
    team = math.lcm(width, HEAD_DIM) // width
    teams = devices // team
    team_heads = team * width // HEAD_DIM
    me = lax.axis_index("seq")
    place = me % team

    selector = (
        mask_ids[:, None] == jnp.arange(mask_table.shape[0], dtype=jnp.int32)[None, :]
    ).astype(jnp.bfloat16)
    condition = (
        control.astype(jnp.float32)
        + jnp.dot(selector, mask_table, preferred_element_type=jnp.float32)
    ).astype(jnp.bfloat16)
    conditions = lax.all_gather(condition, "seq", axis=0, tiled=True, axis_index_groups=[ring])
    residual = jnp.dot(conditions, res_weight, preferred_element_type=jnp.float32).astype(
        jnp.bfloat16
    )
    owner_ring = jnp.concatenate(
        [owner[place_ * row_count : (place_ + 1) * row_count] for place_ in ring]
    )
    relay = (jnp.arange(total_rows, dtype=jnp.int32)[:, None] == owner_ring[None, :]).astype(
        jnp.bfloat16
    )
    by_owner = jnp.dot(relay, residual, preferred_element_type=jnp.float32).astype(jnp.bfloat16)
    relayed = lax.all_to_all(by_owner, "seq", split_axis=0, concat_axis=1, tiled=True)
    hidden = base.astype(jnp.float32) + relayed.astype(jnp.float32)
    normed = layer_norm(hidden, modulation)
    joined = jnp.concatenate([q_weight, k_weight, v_weight], axis=1)
    normed_all = lax.all_gather(normed, "seq", axis=0, tiled=True, axis_index_groups=[ring])
    columns = lax.dot_general(
        joined, normed_all, (((0,), (1,)), ((), ())), preferred_element_type=jnp.float32
    ).astype(jnp.bfloat16)
    team_groups = [[t * team + r for r in range(team)] for t in range(teams)]
    columns = lax.all_gather(columns, "seq", axis=0, axis_index_groups=team_groups)
    columns = columns.reshape(team, 3, width, total_rows).transpose(1, 0, 2, 3)
    columns = columns.reshape(3, team_heads, HEAD_DIM, total_rows)
    spots = jnp.array([ring.index(d) for d in range(devices)], jnp.int32).reshape(teams, team)
    blocks = columns[0].reshape(team_heads, HEAD_DIM, devices, row_count)
    queries = jnp.take(blocks, jnp.take(spots, place, axis=1), axis=2)
    queries = queries.reshape(team_heads, HEAD_DIM, teams * row_count)
    scores = jnp.einsum(
        "hdt,hdk->htk", queries, columns[1], preferred_element_type=jnp.float32
    ) / math.sqrt(HEAD_DIM)
    expo = jnp.exp(scores - jnp.max(scores, axis=2, keepdims=True))
    denom = jnp.sum(expo, axis=2)
    summed = jnp.einsum(
        "htk,hdk->thd",
        expo.astype(jnp.bfloat16),
        columns[2],
        preferred_element_type=jnp.float32,
    )
    mine = (summed / denom.T[:, :, None]).astype(jnp.bfloat16)
    mine = mine.reshape(teams, row_count, team_heads * HEAD_DIM)
    place_groups = [[t * team + r for t in range(teams)] for r in range(team)]
    parts = lax.all_to_all(
        mine, "seq", split_axis=0, concat_axis=0, tiled=True, axis_index_groups=place_groups
    )
    attended = parts.transpose(1, 0, 2).reshape(row_count, teams * team_heads * HEAD_DIM)
    return (hidden.astype(jnp.bfloat16), attended)


VMEM = pl.BlockSpec(memory_space=pltpu.VMEM)
SMEM = pl.BlockSpec(memory_space=pltpu.SMEM)
HBM = pl.BlockSpec(memory_space=pltpu.HBM)
NT = (((1,), (1,)), ((), ()))
LANES = 128
GATHER_BYTES = 1 << 20


def call(kernel, out_shape, in_specs, scratch=(), limit=8 << 20):
    multiple = isinstance(out_shape, (tuple, list))
    return pl.pallas_call(
        kernel,
        out_shape=out_shape,
        in_specs=in_specs,
        out_specs=[VMEM] * len(out_shape) if multiple else VMEM,
        scratch_shapes=list(scratch),
        compiler_params=pltpu.CompilerParams(vmem_limit_bytes=limit),
    )


def matmul_nt(left, right):
    return lax.dot_general(left, right, NT, preferred_element_type=jnp.float32)


def identity(size):
    rows = lax.broadcasted_iota(jnp.int32, (size, size), 0)
    return (rows == lax.broadcasted_iota(jnp.int32, (size, size), 1)).astype(jnp.bfloat16)


def condition_kernel(
    far_ids,
    far_control,
    far_table,
    far_base,
    far_owner,
    block,
    tail,
    owner,
    ids,
    table,
    control,
    base,
    arrived,
):
    copies = [
        pltpu.make_async_copy(source, target, arrived.at[i])
        for i, (source, target) in enumerate(
            (
                (far_ids, ids),
                (far_table, table),
                (far_control, control),
                (far_base, base),
                (far_owner, owner),
            )
        )
    ]
    for copy in copies:
        copy.start()
    rows, model = control.shape
    kinds = table.shape[0]
    head = block.shape[1] - model
    copies[0].wait()
    kind = jnp.zeros((rows, 1), jnp.int32)
    row = lax.broadcasted_iota(jnp.int32, (rows, 1), 0)
    for i in range(rows):
        kind = jnp.where(row == i, ids[i], kind)
    copies[1].wait()
    copies[2].wait()
    entries = table[...].astype(jnp.float32)
    chosen = jnp.broadcast_to(entries[:1], (rows, model))
    for j in range(1, kinds):
        chosen = jnp.where(kind == j, entries[j : j + 1], chosen)
    block[:, :model] = (control[...].astype(jnp.float32) + chosen).astype(jnp.bfloat16)
    copies[3].wait()
    block[:, model:] = base[:, :head]
    for tile in range(tail.shape[0] // rows):
        lanes = slice(head + tile * LANES, head + (tile + 1) * LANES)
        tail[tile * rows : (tile + 1) * rows] = base[:, lanes]
    copies[4].wait()


def holder_of(me, team, block):
    return ((me // team) ^ (block // team)) * team + ((me % team) ^ (block % team))


def natural_rows(me, team, count, rows):
    lane = lax.broadcasted_iota(jnp.int32, (1, rows), 1)
    place = holder_of(me, team, lane // count) * count + lane % count
    row = lax.broadcasted_iota(jnp.int32, (rows, rows), 0)
    return (row == place).astype(jnp.bfloat16)


def stack(blocks, columns):
    return jnp.concatenate([block[:, columns] for block in blocks], axis=0)


def load_kernel(far_weight, weight, arrived):
    copy = pltpu.make_async_copy(far_weight, weight, arrived)
    copy.start()
    copy.wait()


def residual_kernel(team, me, *refs):
    blocks, (weight, owner, tail, out) = refs[:-4], refs[-4:]
    block, model = weight.shape
    rows = owner.shape[1]
    conditions = stack(blocks, slice(model))
    residual = matmul_nt(weight[...], conditions).astype(jnp.bfloat16)
    row = lax.broadcasted_iota(jnp.int32, (rows, rows), 0)
    names = (row == owner[...]).astype(jnp.bfloat16)
    relay = jnp.dot(
        names,
        natural_rows(me[0], team, blocks[0].shape[0], rows),
        preferred_element_type=jnp.float32,
    ).astype(jnp.bfloat16)
    out[:block] = matmul_nt(residual, relay).astype(jnp.bfloat16)
    out[block:] = tail[...]


def fold(values):
    tiles = [values[:, i : i + LANES] for i in range(0, values.shape[1], LANES)]
    return sum(tiles[1:], tiles[0])


def project_kernel(devices, team, me, *refs):
    landed, blocks = refs[:devices], refs[devices : 2 * devices]
    modulation, q_weight, k_weight, v_weight = refs[2 * devices : 2 * devices + 4]
    outs, (hidden_out, hidden, normed, gathered) = refs[2 * devices + 4 : -4], refs[-4:]
    rows, model = hidden.shape
    block = model // devices
    count = hidden_out.shape[0]
    for k, piece in enumerate(landed):
        gathered[holder_of(me[0], team, k)] = piece[...]
    head = blocks[0].shape[1] - model
    turned = natural_rows(me[0], team, count, rows)
    eye = identity(rows)
    pair = 2 * block
    spans = []
    total = jnp.zeros((rows, LANES), jnp.float32)
    squares = jnp.zeros((rows, LANES), jnp.float32)
    for p in range(devices // 2):
        first = 2 * p * block
        lanes = slice(first, first + pair)
        spans.append(lanes)
        relayed = jnp.concatenate([gathered[2 * p, :block], gathered[2 * p + 1, :block]], axis=0)
        if first < head:
            there = slice(model + first, model + first + pair)
            placed = jnp.dot(
                turned,
                stack(blocks, there),
                preferred_element_type=jnp.float32,
            )
        else:
            for tile in range(pair // LANES):
                at = first + tile * LANES
                row = block + (at - head) // LANES * count
                for device in range(devices):
                    hidden[device * count : (device + 1) * count, at : at + LANES] = gathered[
                        device, row : row + count
                    ].astype(jnp.float32)
            placed = hidden[:, lanes]
        summed = placed + matmul_nt(eye, relayed)
        hidden[:, lanes] = summed
        if p == 0:
            near = jnp.sum(fold(summed), axis=1, keepdims=True) * (1.0 / pair)
        apart = summed - near
        total = total + fold(apart)
        squares = squares + fold(apart * apart)
    shift = jnp.sum(total, axis=1, keepdims=True) * (1.0 / model)
    mean = near + shift
    spread = jnp.sum(squares, axis=1, keepdims=True) * (1.0 / model) - shift * shift
    inverse = lax.rsqrt(spread + 1e-06)
    for lanes in spans:
        scaled = ((hidden[:, lanes] - mean) * inverse) * (1.0 + modulation[1:2, lanes])
        normed[:, lanes] = (scaled + modulation[0:1, lanes]).astype(jnp.bfloat16)
    first = pl.multiple_of(me[0] * count, count)
    hidden_out[...] = hidden[pl.ds(first, count), :].astype(jnp.bfloat16)
    weights = jnp.concatenate([q_weight[...], k_weight[...], v_weight[...]], axis=0)
    columns = matmul_nt(weights, normed[...]).astype(jnp.bfloat16)
    width = q_weight.shape[0]
    place = lax.broadcasted_iota(jnp.int32, (rows, rows), 0)
    each = rows // team
    member = (me[0] % team) ^ (place // each)
    there = (me[0] // team) ^ (place % each // count)
    wanted = (there * team + member) * count + place % count
    pick = (wanted == lax.broadcasted_iota(jnp.int32, (rows, rows), 1)).astype(jnp.bfloat16)
    queries = matmul_nt(pick, columns[:width]).astype(jnp.bfloat16)
    for k, out in enumerate(outs):
        out[: 2 * width] = columns[width:]
        out[2 * width :, :width] = queries[k * each : (k + 1) * each]
        out[2 * width :, width:] = jnp.zeros((each, rows - width), jnp.bfloat16)


def attend_kernel(team, teams, me, *refs):
    arrived, outs, held = refs[:team], refs[team : team + teams], refs[-1]
    count = outs[0].shape[0]
    width = outs[0].shape[1] // team
    place = me[0] % team
    for k in range(team):
        held[place ^ k] = arrived[k][...]
    keys = jnp.concatenate([held[r, :width] for r in range(team)], axis=0)
    values = jnp.concatenate([held[r, width : 2 * width] for r in range(team)], axis=0)
    queries = jnp.concatenate([held[r, 2 * width :, :width] for r in range(team)], axis=1)
    for h in range(team * width // HEAD_DIM):
        span = slice(h * HEAD_DIM, (h + 1) * HEAD_DIM)
        scores = jnp.dot(
            queries[:, span], keys[span], preferred_element_type=jnp.float32
        ) / math.sqrt(HEAD_DIM)
        expo = jnp.exp(scores - jnp.max(scores, axis=1, keepdims=True))
        denom = jnp.sum(expo, axis=1, keepdims=True)
        mixed = matmul_nt(expo.astype(jnp.bfloat16), values[span]) / denom
        for k, out in enumerate(outs):
            out[:, span] = mixed[k * count : (k + 1) * count].astype(jnp.bfloat16)


def gather_kernel(team, me, *refs):
    blocks, out = refs[:-1], refs[-1]
    columns = blocks[0].shape[1]
    for k, block in enumerate(blocks):
        first = pl.multiple_of(((me[0] // team) ^ k) * columns, columns)
        out[:, pl.ds(first, columns)] = block[...]


def exchange(values, devices, step):
    return lax.ppermute(values, "seq", [(d, d ^ step) for d in range(devices)])


def gather(values, devices, team):
    blocks = {0: values}
    steps = [k * team for k in range(1, devices // team)]
    for step in steps:
        blocks[step] = exchange(values, devices, step)
    step = team // 2
    while step:
        for k in list(blocks):
            blocks[k + step] = exchange(blocks[k], devices, step)
        step //= 2
    return [blocks[k] for k in range(devices)]


def on_device(
    devices,
    control,
    mask_ids,
    owner,
    mask_table,
    res_weight,
    base,
    modulation,
    q_weight,
    k_weight,
    v_weight,
):
    count, model = base.shape
    rows = owner.shape[0]
    block = res_weight.shape[1]
    width = q_weight.shape[1]
    team = math.lcm(width, HEAD_DIM) // width
    teams = devices // team
    me = lax.axis_index("seq")
    bf16 = jnp.bfloat16
    shape = jax.ShapeDtypeStruct

    tiles = ((GATHER_BYTES - 1) // (2 * devices * rows) - block) // count
    tiles -= tiles % (2 * block // LANES)
    head = model - tiles * LANES

    inputs = (mask_ids, control, mask_table, base, owner.reshape(1, rows))
    mine, tail, near_owner = call(
        condition_kernel,
        (
            pltpu.VMEM((count, model + head), bf16),
            pltpu.VMEM((tiles * count, LANES), bf16),
            pltpu.VMEM((1, rows), jnp.int32),
        ),
        [HBM] * len(inputs),
        [
            pltpu.SMEM((count,), jnp.int32),
            pltpu.VMEM(mask_table.shape, bf16),
            pltpu.VMEM((count, model), bf16),
            pltpu.VMEM((count, model), bf16),
            pltpu.SemaphoreType.DMA((len(inputs),)),
        ],
    )(*[pltpu.with_memory_space_constraint(x, pltpu.HBM) for x in inputs])
    blocks = gather(mine, devices, team)
    near_weight = call(
        load_kernel,
        pltpu.VMEM((block, model), bf16),
        [HBM],
        [pltpu.SemaphoreType.DMA],
    )(pltpu.with_memory_space_constraint(res_weight.T, pltpu.HBM))
    payload = call(
        functools.partial(residual_kernel, team),
        shape((block + tiles * count, rows), bf16),
        [SMEM] + [VMEM] * (len(blocks) + 3),
    )(me.reshape(1), *blocks, near_weight, near_owner, tail)
    landed = gather(payload, devices, team)
    each = teams * count
    *columns, hidden_out = call(
        functools.partial(project_kernel, devices, team),
        tuple(shape((2 * width + each, rows), bf16) for _ in range(team))
        + (shape((count, model), bf16),),
        [SMEM] + [VMEM] * (2 * devices + 4),
        [
            pltpu.VMEM((rows, model), jnp.float32),
            pltpu.VMEM((rows, model), bf16),
            pltpu.VMEM((devices,) + payload.shape, bf16),
        ],
    )(me.reshape(1), *landed, *blocks, modulation, q_weight.T, k_weight.T, v_weight.T)
    head_columns = team * width
    arrived = [columns[0]]
    for k in range(1, team):
        arrived.append(exchange(columns[k], devices, k))
    results = call(
        functools.partial(attend_kernel, team, teams),
        tuple(shape((count, head_columns), bf16) for _ in range(teams)),
        [SMEM] + [VMEM] * team,
        [pltpu.VMEM((team, 2 * width + each, rows), bf16)],
    )(me.reshape(1), *arrived)
    crossed = {}
    for k in range(1, teams):
        crossed[k] = exchange(results[k], devices, k * team)
    parts = [results[0]] + [crossed[k] for k in range(1, teams)]
    attended = call(
        functools.partial(gather_kernel, team),
        shape((count, teams * head_columns), bf16),
        [SMEM] + [VMEM] * teams,
    )(me.reshape(1), *parts)
    return (hidden_out, attended)


def fits(devices, rows, block, width):
    team = math.lcm(width, HEAD_DIM) // width
    powers = all(n & (n - 1) == 0 for n in (devices, team))
    return rows == LANES and devices > team > 1 and powers and block % 64 == 0 and width % 16 == 0


def on_any_device(devices, *arguments):
    owner, res_weight, q_weight = arguments[2], arguments[4], arguments[7]
    tidy = fits(devices, owner.shape[0], res_weight.shape[1], q_weight.shape[1])
    return (on_device if tidy else on_device_plain)(devices, *arguments)


def solution(mesh):
    in_specs = (
        P(("parts", "seq"), None),
        P(("parts", "seq")),
        P("parts"),
        P(),
        P(None, "seq"),
        P(("parts", "seq"), None),
        P(),
        P(None, "seq"),
        P(None, "seq"),
        P(None, "seq"),
    )
    out_specs = (P(("parts", "seq"), None), P(("parts", "seq"), None))
    return jax.shard_map(
        functools.partial(on_any_device, mesh.shape["seq"]),
        mesh=mesh,
        in_specs=in_specs,
        out_specs=out_specs,
        check_vma=False,
    )
```
